32 devices in a mesh: section: 8 (over z, y), dp: 4 (over x, core).
Axes of the slice: x: 2, y: 2, z: 4, core: 2. Of those that a mesh axis runs over, the one named last changes fastest.
Arguments:
- tokens: bfloat16 [4, 4, 128, 768], P(None, 'dp'), may hold values from -6 to 6
- cotangent: bfloat16 [4, 4, 128, 768], P(None, 'dp'), may hold values from -6 to 6
- document_lengths: int32 [4, 4, 4], P(None, 'dp'), may hold values from 1 to 64, 128 in all within a row
- valid_counts: int32 [4, 4], P(None, 'dp'), may hold values from 64 to 128
- first_gain: bfloat16 [16, 768], P('section'), may hold values from 0.5 to 1.5
- first_shift: bfloat16 [16, 768], P('section'), may hold values from -1 to 1
- joint_weight: bfloat16 [16, 768, 2304], P('section'), may hold values from -0.21875 to 0.21875
- query_value_offsets: bfloat16 [16, 1536], P('section'), may hold values from -1 to 1
- output_weight: bfloat16 [16, 768, 768], P('section'), may hold values from -0.625 to 0.625
- output_bias: bfloat16 [16, 768], P('section'), may hold values from -1 to 1
- second_gain: bfloat16 [16, 768], P('section'), may hold values from 0.5 to 1.5
- second_shift: bfloat16 [16, 768], P('section'), may hold values from -1 to 1
- expand_weight: bfloat16 [16, 768, 3072], P('section'), may hold values from -0.21875 to 0.21875
- expand_bias: bfloat16 [16, 3072], P('section'), may hold values from -1 to 1
- contract_weight: bfloat16 [16, 3072, 768], P('section'), may hold values from -0.109375 to 0.109375
- contract_bias: bfloat16 [16, 768], P('section'), may hold values from -1 to 1
Outputs:
- final_hidden: float32 [4, 4, 128, 768], P(None, 'dp', None, 'section')
- input_gradient: float32 [4, 4, 128, 768], P(None, 'dp', None, 'section')
- first_gain_gradient: float32 [16, 768], P('section', 'dp')
- first_shift_gradient: float32 [16, 768], P('section', 'dp')
- joint_weight_gradient: float32 [16, 768, 2304], P('section', 'dp')
- query_value_bias_gradient: float32 [16, 1536], P('section', 'dp')
- output_weight_gradient: float32 [16, 768, 768], P('section', 'dp')
- output_bias_gradient: float32 [16, 768], P('section', 'dp')
- second_gain_gradient: float32 [16, 768], P('section', 'dp')
- second_shift_gradient: float32 [16, 768], P('section', 'dp')
- expand_weight_gradient: float32 [16, 768, 3072], P('section', 'dp')
- expand_bias_gradient: float32 [16, 3072], P('section', 'dp')
- contract_weight_gradient: float32 [16, 3072, 768], P('section', 'dp')
- contract_bias_gradient: float32 [16, 768], P('section', 'dp')
The draws below stay inside these ranges and needn't reach their ends.
Inputs may be any that keep to these rules, and one draw needn't show every extreme that they name: `document_lengths`: the 4 document lengths of a row sum to 128.
All inputs are finite; a program needn't handle non-finite values.
Results may differ from the reference program's by a relative error of at most 0.024.
Values sent between devices are 32-bit elements; how exact they have to be, the bound alone decides.
No kernel may reach another device: no remote copies, remote signals or barrier semaphores. Data moves between devices by JAX's collectives and lax.ppermute only.
A program may use at most 256 MiB of HBM per device.

```python
import math
from functools import partial
import jax
import jax.numpy as jnp
import numpy as np
from jax import lax

D = 768
HEAD_DIM = 64
FF = 3072
LAYERS = 2
MICRO = 4
LEN = 128
DOCS = 4
BATCH = 4
DEPTH = 16
N_SECTION = 8


def draw_valid_counts(key, part):
    counts = jax.random.randint(key, (MICRO, BATCH), LEN // 2, LEN + 1, dtype=jnp.int32)
    counts = counts.at[0, 0].set(LEN)
    return counts.at[MICRO - 1, BATCH - 1].set(LEN // 2)


def block_levels(key, shape, shards, low, largest):
    def one(axis_at, parts):
        heights = jax.random.uniform(jax.random.fold_in(jax.random.fold_in(key, 6), axis_at), (parts,), jnp.float32, low / len(shards), largest / len(shards))
        return jnp.repeat(jnp.exp(heights), shape[axis_at] // parts).reshape((-1,) + (1,) * (len(shape) - axis_at - 1))

    loudness = one(*shards[0])
    for cut in shards[1:]:
        loudness = loudness * one(*cut)
    return loudness


def split_up(amount, total, limit, slope):
    portions = [(1 << 20) // math.isqrt(grade ** slope) + 1 for grade in range(2, amount + 1)]
    spare, holding = total - limit - (amount - 1), [1] * (amount - 1)
    while spare > 0:
        candidates = [i for i in range(amount - 1) if holding[i] < limit]
        pool, left = sum([portions[i] for i in candidates]), spare
        for i in candidates:
            addition = min(limit - holding[i], max(1, left * portions[i] // pool), spare)
            holding[i] = holding[i] + addition
            spare = spare - addition
    return np.array([limit] + holding)


def uneven(key, count, total, limit, lean):
    if count == 2:
        one = jax.random.randint(key, (), max(1, total - limit), min(limit, total - 1) + 1)
        return jnp.stack([one, total - one])
    lengths = jnp.asarray(split_up(count, total, limit, lean), jnp.int32)
    pairs = (count - 1) // 2
    source_of, sink = lengths[1:1 + 2 * pairs:2], lengths[2:2 + 2 * pairs:2]
    slack = jnp.minimum(source_of - 1, limit - sink)
    shifted = jax.random.randint(jax.random.fold_in(key, 1), (pairs,), 0, 1 << 20) % (slack + 1)
    lengths = lengths.at[1:1 + 2 * pairs:2].set(source_of - shifted).at[2:2 + 2 * pairs:2].set(sink + shifted)
    return lengths[jax.random.permutation(jax.random.fold_in(key, 2), count)]


def gaussian(stream_key, shape, deviation, bound, cuts=(), held_as=jnp.bfloat16):
    values = deviation * jax.random.normal(stream_key, shape, jnp.float32)
    if cuts:
        values = values * block_levels(stream_key, shape, cuts, -0.22, 0.18)
    return jnp.clip(values, -bound, bound).astype(held_as)


def setup_inputs(seed: int = 0) -> dict:
    key_list = jax.random.split(jax.random.key(seed), 17)
    tokens = gaussian(key_list[0], (MICRO, BATCH, LEN, D), 1.0, 6.0, ((1, 4),))
    cotangent = gaussian(key_list[1], (MICRO, BATCH, LEN, D), 1.0, 6.0, ((1, 4),))
    document_lengths = jax.vmap(lambda own: uneven(own, DOCS, LEN, LEN // 2, 2))(jax.random.split(key_list[2], MICRO * BATCH)).reshape((MICRO, BATCH, DOCS)).astype(jnp.int32)
    valid_counts = draw_valid_counts(jax.random.fold_in(key_list[16], 71), 0)
    first_gain = jnp.clip(1.0 + 0.1 * jax.random.normal(key_list[4], (DEPTH, D), jnp.float32), 0.5, 1.5).astype(jnp.bfloat16)
    first_shift = gaussian(key_list[5], (DEPTH, D), 0.2, 1.0, ((0, 8),))
    joint_weight = gaussian(key_list[6], (DEPTH, D, 3 * D), D ** -0.5, 0.21875, ((0, 8),))
    query_value_offsets = gaussian(key_list[7], (DEPTH, 2 * D), 0.2, 1.0, ((0, 8),))
    output_weight = gaussian(key_list[8], (DEPTH, D, D), (D // 8) ** -0.5, 0.625, ((0, 8),))
    output_bias = gaussian(key_list[9], (DEPTH, D), 0.2, 1.0, ((0, 8),))
    second_gain = jnp.clip(1.0 + 0.1 * jax.random.normal(key_list[10], (DEPTH, D), jnp.float32), 0.5, 1.5).astype(jnp.bfloat16)
    second_shift = gaussian(key_list[11], (DEPTH, D), 0.2, 1.0, ((0, 8),))
    expand_weight = gaussian(key_list[12], (DEPTH, D, FF), D ** -0.5, 0.21875, ((0, 8),))
    expand_bias = gaussian(key_list[13], (DEPTH, FF), 0.2, 1.0, ((0, 8),))
    contract_weight = gaussian(key_list[14], (DEPTH, FF, D), FF ** -0.5, 0.109375, ((0, 8),))
    contract_bias = gaussian(key_list[15], (DEPTH, D), 0.2, 1.0, ((0, 8),))
    return {"tokens": tokens, "cotangent": cotangent, "document_lengths": document_lengths, "valid_counts": valid_counts, "first_gain": first_gain, "first_shift": first_shift, "joint_weight": joint_weight, "query_value_offsets": query_value_offsets, "output_weight": output_weight, "output_bias": output_bias, "second_gain": second_gain, "second_shift": second_shift, "expand_weight": expand_weight, "expand_bias": expand_bias, "contract_weight": contract_weight, "contract_bias": contract_bias}


@jax.custom_vjp
def low(v):
    return lax.optimization_barrier(v.astype(jnp.bfloat16)).astype(jnp.float32)

@jax.custom_vjp
def low_back(v):
    return v

def low_keep(v):
    return (low(v), None)

def low_pass(kept, grad):
    return (grad,)

def back_keep(v):
    return (v, None)

def back_low(kept, grad):
    return (low(grad),)
low.defvjp(low_keep, low_pass)
low_back.defvjp(back_keep, back_low)

def layer_norm(values, gain, offset):
    center = lax.optimization_barrier(jnp.mean(values, axis=-1, keepdims=True))
    centered = values - center
    spread = lax.optimization_barrier(jnp.mean(centered * centered, axis=-1, keepdims=True))
    return centered * lax.rsqrt(spread + 1e-05) * gain + offset

def both_round(values):
    return low(low_back(values))

def project(left_operand, right_operand):
    return jnp.einsum('rjp,pu->rju', left_operand, right_operand, precision=lax.Precision.HIGHEST)

def attend(joint, allowed):
    seq_count, length, triple = joint.shape
    feature_count = triple // 3
    pieces = joint.reshape(seq_count, length, 3, feature_count // HEAD_DIM, HEAD_DIM)
    queries = pieces[:, :, 0]
    keys_all = pieces[:, :, 1]
    gathered_values = pieces[:, :, 2]
    scores = jnp.einsum('sqhd,skhd->shqk', queries, keys_all, precision=lax.Precision.HIGHEST) * HEAD_DIM ** (-0.5)
    scores = low_back(scores)
    masked = jnp.where(allowed[:, None], scores, -1e+30)
    probabilities = low(jax.nn.softmax(masked, axis=-1))
    mixture = jnp.einsum('shqk,skhd->sqhd', probabilities, gathered_values, precision=lax.Precision.HIGHEST)
    return mixture.reshape(seq_count, length, feature_count)

def one_layer(hidden, params, allowed, branch_scale):
    first_gain, first_shift, joint_weight, query_value_offsets, output_weight, output_bias, second_gain, second_shift, expand_weight, expand_bias, contract_weight, contract_bias = params
    feature_count = hidden.shape[-1]
    normed = low(layer_norm(hidden, first_gain, first_shift))
    bias_full = jnp.concatenate([query_value_offsets[:feature_count], jnp.zeros_like(query_value_offsets[:feature_count]), query_value_offsets[feature_count:]])
    joint = both_round(project(normed, joint_weight) + bias_full)
    attended = both_round(attend(joint, allowed))
    after_attention = hidden + branch_scale * low_back(project(attended, output_weight) + output_bias)
    second = low(layer_norm(after_attention, second_gain, second_shift))
    hidden_pre = low_back(project(second, expand_weight) + expand_bias)
    activated = low(jax.nn.gelu(hidden_pre, approximate=True))
    return after_attention + branch_scale * low_back(project(activated, contract_weight) + contract_bias)

def run_layers(hidden, weights, allowed):
    branch_scale = (LAYERS * N_SECTION) ** (-0.5)
    layer_step = jax.checkpoint(partial(one_layer, allowed=allowed, branch_scale=branch_scale))

    def advance(carry, params):
        return (layer_step(carry, params), None)
    final, _ = lax.scan(advance, hidden, weights)
    return final

def reference(tokens, cotangent, document_lengths, valid_counts, first_gain, first_shift, joint_weight, query_value_offsets, output_weight, output_bias, second_gain, second_shift, expand_weight, expand_bias, contract_weight, contract_bias):
    micro_count, batch_count, length, feature_count = tokens.shape
    seq_count = micro_count * batch_count
    positions = jnp.arange(length, dtype=jnp.int32)
    document_ends = jnp.cumsum(document_lengths.reshape(seq_count, DOCS), axis=-1).astype(jnp.int32)
    segment = lax.optimization_barrier(jnp.sum((positions[None, :, None] >= document_ends[:, None, :]).astype(jnp.int32), axis=-1))
    causal = positions[:, None] >= positions[None, :]
    allowed = (segment[:, :, None] == segment[:, None, :]) & causal[None]
    live_tokens = (positions[None, :] < valid_counts.reshape(seq_count, 1)).astype(jnp.float32)
    weights = tuple((array.astype(jnp.float32) for array in (first_gain, first_shift, joint_weight, query_value_offsets, output_weight, output_bias, second_gain, second_shift, expand_weight, expand_bias, contract_weight, contract_bias)))
    start = tokens.astype(jnp.float32).reshape(seq_count, length, feature_count)
    final, pullback = jax.vjp(partial(run_layers, allowed=allowed), start, weights)
    seed_gradient = cotangent.astype(jnp.float32).reshape(start.shape) * live_tokens[:, :, None]
    input_gradient, gradients = pullback(seed_gradient)
    return (final.reshape(tokens.shape), input_gradient.reshape(tokens.shape), gradients[0], gradients[1], gradients[2], gradients[3], gradients[4], gradients[5], gradients[6], gradients[7], gradients[8], gradients[9], gradients[10], gradients[11])
```

```python
from functools import partial

import jax
import jax.numpy as jnp
from jax import lax
from jax.experimental import pallas as pl
from jax.experimental.pallas import tpu as pltpu
from jax.sharding import PartitionSpec as P

HEAD_DIM = 64
LAYERS = 2
PAIR = 2 * HEAD_DIM
CHUNK = 768
EPS = 1e-05
BF16 = jnp.bfloat16
F32 = jnp.float32
ANY = pl.BlockSpec(memory_space=pl.ANY)
SMEM = pl.BlockSpec(memory_space=pltpu.SMEM)
TANH_SCALE = 0.7978845608028654


def mm(left, right):
    return lax.dot_general(left, right, (((1,), (0,)), ((), ())), preferred_element_type=F32)


def mm_nt(left, right):
    return lax.dot_general(left, right, (((1,), (1,)), ((), ())), preferred_element_type=F32)


def mm_tn(left, right):
    return lax.dot_general(left, right, (((0,), (0,)), ((), ())), preferred_element_type=F32)


def norm_parts(values):
    center = jnp.mean(values, axis=-1, keepdims=True)
    centered = values - center
    scale = lax.rsqrt(jnp.mean(centered * centered, axis=-1, keepdims=True) + EPS)
    return centered * scale, scale


def norm_back(normed, scale, gain, gradient):
    weighted = gradient * gain
    mean_weighted = jnp.mean(weighted, axis=-1, keepdims=True)
    mean_product = jnp.mean(weighted * normed, axis=-1, keepdims=True)
    return scale * (weighted - mean_weighted - normed * mean_product)


def stack_halves(block):
    low_lanes = lax.broadcasted_iota(jnp.int32, block.shape, 1) < HEAD_DIM
    zero = jnp.zeros_like(block)
    return jnp.concatenate(
        [jnp.where(low_lanes, block, zero), jnp.where(low_lanes, zero, block)], axis=0
    )


def join_halves(stacked):
    length = stacked.shape[0] // 2
    low_lanes = lax.broadcasted_iota(jnp.int32, (length, PAIR), 1) < HEAD_DIM
    return jnp.where(low_lanes, stacked[:length], stacked[length:])


def pair_probabilities(queries, keys, allowed):
    scores = mm_nt(queries, keys) * HEAD_DIM ** (-0.5)
    scores = jnp.where(allowed, scores, -1e30)
    powers = jnp.exp(scores - jnp.max(scores, axis=-1, keepdims=True))
    return powers / jnp.sum(powers, axis=-1, keepdims=True)


def column_sum(values):
    return jnp.sum(values.astype(F32), axis=0, keepdims=True)


def forward_kernel(
    branch_scale,
    flags,
    tokens,
    arrived,
    allowed_rows,
    wj,
    wo,
    we,
    wc,
    vecs,
    bj,
    be,
    *refs,
):
    names = ("h", "g", "a", "t", "o", "c", "m", "d", "f")
    stash = dict(zip(names, refs[9:18]))
    sent = refs[18]
    (
        wj_v,
        wo_v,
        we_v,
        wc_v,
        vecs_v,
        bj_v,
        be_v,
        allow_v,
        h_v,
        g_v,
        a_v,
        t_v,
        o_v,
        c_v,
        m_v,
        d_v,
        w_sem,
        in_sem,
        out_sem,
    ) = refs[19:]
    active, slot, first, last = flags[0], flags[1], flags[2], flags[3]
    feature = h_v.shape[-1]
    hidden = we_v.shape[-1]

    @pl.when(active == 1)
    def _():
        small = [
            pltpu.make_async_copy(allowed_rows.at[slot], allow_v, in_sem.at[1]),
            pltpu.make_async_copy(vecs, vecs_v, in_sem.at[2]),
            pltpu.make_async_copy(bj, bj_v, in_sem.at[3]),
            pltpu.make_async_copy(be, be_v, in_sem.at[4]),
        ]

        @pl.when(first == 1)
        def _():
            pltpu.make_async_copy(tokens.at[slot], h_v.at[0], in_sem.at[0]).start()

        @pl.when(first == 0)
        def _():
            pltpu.make_async_copy(arrived, h_v.at[0], in_sem.at[0]).start()

        for copy in small:
            copy.start()
        sources = ((wj, wj_v), (wo, wo_v), (we, we_v), (wc, wc_v))
        for layer in range(LAYERS):
            for index, (source, target) in enumerate(sources):
                pltpu.make_async_copy(
                    source.at[layer], target.at[layer], w_sem.at[layer, index]
                ).start()

        def weight_wait(layer, index):
            source, target = sources[index]
            pltpu.make_async_copy(
                source.at[layer], target.at[layer], w_sem.at[layer, index]
            ).wait()

        def put(layer, index, name, value_ref):
            return pltpu.make_async_copy(
                value_ref.at[layer], stash[name].at[layer, slot], out_sem.at[layer, index]
            )

        pltpu.make_async_copy(arrived, h_v.at[0], in_sem.at[0]).wait()
        for copy in small:
            copy.wait()
        allowed = allow_v[...] > 0.5
        allowed = jnp.concatenate([allow_v[...], allow_v[...]], axis=0) > 0.5

        for layer in range(LAYERS):
            put(layer, 0, "h", h_v).start()
            row = h_v[layer]
            normed, _ = norm_parts(row)
            a_low = (
                normed * vecs_v[layer, 0:1, :] + vecs_v[layer, 1:2, :]
            ).astype(BF16)
            a_v[layer] = a_low
            put(layer, 2, "a", a_v).start()
            weight_wait(layer, 0)
            for start in range(0, 3 * feature, CHUNK):
                span = slice(start, start + CHUNK)
                t_v[layer, :, span] = (
                    mm(a_low, wj_v[layer, :, span]) + bj_v[layer, :, span]
                ).astype(BF16)
            put(layer, 3, "t", t_v).start()
            for start in range(0, feature, PAIR):
                queries = stack_halves(t_v[layer, :, start : start + PAIR])
                keys = t_v[layer, :, feature + start : feature + start + PAIR]
                values = t_v[layer, :, 2 * feature + start : 2 * feature + start + PAIR]
                chances = pair_probabilities(queries, keys, allowed).astype(BF16)
                o_v[layer, :, start : start + PAIR] = join_halves(mm(chances, values)).astype(BF16)
            put(layer, 4, "o", o_v).start()
            weight_wait(layer, 1)
            mixed = row + branch_scale * (mm(o_v[layer], wo_v[layer]) + vecs_v[layer, 2:3, :])
            g_v[layer] = mixed
            put(layer, 1, "g", g_v).start()
            normed, _ = norm_parts(mixed)
            c_low = (normed * vecs_v[layer, 3:4, :] + vecs_v[layer, 4:5, :]).astype(BF16)
            c_v[layer] = c_low
            put(layer, 5, "c", c_v).start()
            weight_wait(layer, 2)
            for start in range(0, hidden, CHUNK):
                span = slice(start, start + CHUNK)
                u = mm(c_low, we_v[layer, :, span]) + be_v[layer, :, span]
                square = u * u
                th = jnp.tanh(TANH_SCALE * (u + 0.044715 * (square * u)))
                half = 0.5 * (1.0 + th)
                m_v[layer, :, span] = (u * half).astype(BF16)
                slope = half + 0.5 * u * (1.0 - th * th) * (
                    TANH_SCALE * (1.0 + 3.0 * 0.044715 * square)
                )
                d_v[layer, :, span] = slope.astype(BF16)
            put(layer, 6, "m", m_v).start()
            put(layer, 7, "d", d_v).start()
            weight_wait(layer, 3)
            output = mixed + branch_scale * (mm(m_v[layer], wc_v[layer]) + vecs_v[layer, 5:6, :])
            h_v[layer + 1] = output
        out = pltpu.make_async_copy(h_v.at[LAYERS], sent, in_sem.at[0])
        out.start()

        @pl.when(last == 1)
        def _():
            final = pltpu.make_async_copy(h_v.at[LAYERS], stash["f"].at[slot], in_sem.at[1])
            final.start()
            final.wait()

        for layer in range(LAYERS):
            for index, (name, value_ref) in enumerate(
                (
                    ("h", h_v),
                    ("g", g_v),
                    ("a", a_v),
                    ("t", t_v),
                    ("o", o_v),
                    ("c", c_v),
                    ("m", m_v),
                    ("d", d_v),
                )
            ):
                put(layer, index, name, value_ref).wait()
        out.wait()


def forward_step(branch_scale, flags, tokens, arrived, allowed, weights, vectors, stash):
    length, feature = arrived.shape
    wj, wo, we, wc = weights
    vecs, bj, be = vectors
    hidden = we.shape[-1]
    params = (wj, wo, we, wc, vecs, bj, be)
    scratch = [
        pltpu.VMEM(wj.shape, BF16),
        pltpu.VMEM(wo.shape, BF16),
        pltpu.VMEM(we.shape, BF16),
        pltpu.VMEM(wc.shape, BF16),
        pltpu.VMEM(vecs.shape, F32),
        pltpu.VMEM(bj.shape, F32),
        pltpu.VMEM(be.shape, F32),
        pltpu.VMEM((length, length), F32),
        pltpu.VMEM((LAYERS + 1, length, feature), F32),
        pltpu.VMEM((LAYERS, length, feature), F32),
        pltpu.VMEM((LAYERS, length, feature), BF16),
        pltpu.VMEM((LAYERS, length, 3 * feature), BF16),
        pltpu.VMEM((LAYERS, length, feature), BF16),
        pltpu.VMEM((LAYERS, length, feature), BF16),
        pltpu.VMEM((LAYERS, length, hidden), BF16),
        pltpu.VMEM((LAYERS, length, hidden), BF16),
        pltpu.SemaphoreType.DMA((LAYERS, 4)),
        pltpu.SemaphoreType.DMA((5,)),
        pltpu.SemaphoreType.DMA((LAYERS, 8)),
    ]
    leading = 4 + len(params)
    outs = pl.pallas_call(
        partial(forward_kernel, branch_scale),
        out_shape=tuple(jax.ShapeDtypeStruct(s.shape, s.dtype) for s in stash)
        + (jax.ShapeDtypeStruct((length, feature), F32),),
        in_specs=[SMEM] + [ANY] * (leading - 1 + len(stash)),
        out_specs=tuple([ANY] * (len(stash) + 1)),
        scratch_shapes=scratch,
        input_output_aliases={leading + i: i for i in range(len(stash))},
        compiler_params=pltpu.CompilerParams(vmem_limit_bytes=56 * 1024 * 1024),
        cost_estimate=pl.CostEstimate(
            flops=2 * length * sum(w.size for w in weights),
            bytes_accessed=2 * sum(w.size for w in weights),
            transcendentals=0,
        ),
        name="forward_step",
    )(flags, tokens, arrived, allowed, *params, *stash)
    return outs[:-1], outs[-1]


def backward_kernel(
    branch_scale,
    flags,
    seeds,
    arrived,
    allowed_rows,
    wj,
    wo,
    we,
    wc,
    vecs,
    sh,
    sg,
    st,
    sd,
    *refs,
):
    names = ("gw", "gu", "gz", "gt", "small", "r")
    stash = dict(zip(names, refs[6:12]))
    sent = refs[12]
    (
        wj_v,
        wo_v,
        we_v,
        wc_v,
        vecs_v,
        allow_v,
        h_v,
        g_v,
        t_v,
        d_v,
        grad_v,
        gw_v,
        gu_v,
        gz_v,
        go_v,
        gt_v,
        small_v,
        w_sem,
        in_sem,
        s_sem,
        out_sem,
    ) = refs[13:]
    active, slot, first, last = flags[0], flags[1], flags[2], flags[3]
    feature = h_v.shape[-1]
    hidden = we_v.shape[-1]

    @pl.when(active == 1)
    def _():
        small = [
            pltpu.make_async_copy(allowed_rows.at[slot], allow_v, in_sem.at[1]),
            pltpu.make_async_copy(vecs, vecs_v, in_sem.at[2]),
        ]

        @pl.when(last == 1)
        def _():
            pltpu.make_async_copy(seeds.at[slot], grad_v, in_sem.at[0]).start()

        @pl.when(last == 0)
        def _():
            pltpu.make_async_copy(arrived, grad_v, in_sem.at[0]).start()

        for copy in small:
            copy.start()
        sources = ((wc, wc_v), (we, we_v), (wo, wo_v), (wj, wj_v))
        saved = ((sd, d_v), (sg, g_v), (st, t_v), (sh, h_v))

        def weight_copy(layer, index):
            source, target = sources[index]
            return pltpu.make_async_copy(
                source.at[layer], target.at[layer], w_sem.at[layer, index]
            )

        def saved_copy(layer, index):
            source, target = saved[index]
            return pltpu.make_async_copy(
                source.at[layer, slot], target.at[layer], s_sem.at[layer, index]
            )

        for layer in reversed(range(LAYERS)):
            for index in range(4):
                weight_copy(layer, index).start()
                saved_copy(layer, index).start()

        def put(layer, index, name, value_ref):
            return pltpu.make_async_copy(
                value_ref.at[layer], stash[name].at[layer, slot], out_sem.at[layer, index]
            )

        pltpu.make_async_copy(arrived, grad_v, in_sem.at[0]).wait()
        for copy in small:
            copy.wait()
        allowed = jnp.concatenate([allow_v[...], allow_v[...]], axis=0) > 0.5

        for layer in reversed(range(LAYERS)):
            gw = (branch_scale * grad_v[...]).astype(BF16)
            gw_v[layer] = gw
            put(layer, 0, "gw", gw_v).start()
            small_v[layer, 7:8, :] = column_sum(gw)
            weight_copy(layer, 0).wait()
            saved_copy(layer, 0).wait()
            for index, start in enumerate(range(0, hidden, CHUNK)):
                span = slice(start, start + CHUNK)
                gu = (
                    d_v[layer, :, span].astype(F32) * mm_nt(gw, wc_v[layer, span, :])
                ).astype(BF16)
                gu_v[layer, :, span] = gu
                small_v[layer, 8 + index : 9 + index, :] = column_sum(gu)
            put(layer, 1, "gu", gu_v).start()
            weight_copy(layer, 1).wait()
            gc = mm_nt(gu_v[layer], we_v[layer])
            saved_copy(layer, 1).wait()
            normed, scale = norm_parts(g_v[layer])
            small_v[layer, 4:5, :] = column_sum(gc * normed)
            small_v[layer, 5:6, :] = column_sum(gc)
            gg = grad_v[...] + norm_back(normed, scale, vecs_v[layer, 3:4, :], gc)
            grad_v[...] = gg
            gz = (branch_scale * gg).astype(BF16)
            gz_v[layer] = gz
            put(layer, 2, "gz", gz_v).start()
            small_v[layer, 6:7, :] = column_sum(gz)
            weight_copy(layer, 2).wait()
            go_v[...] = mm_nt(gz, wo_v[layer]).astype(BF16)
            saved_copy(layer, 2).wait()
            for start in range(0, feature, PAIR):
                queries = stack_halves(t_v[layer, :, start : start + PAIR])
                keys = t_v[layer, :, feature + start : feature + start + PAIR]
                values = t_v[layer, :, 2 * feature + start : 2 * feature + start + PAIR]
                go = stack_halves(go_v[:, start : start + PAIR])
                chances = pair_probabilities(queries, keys, allowed)
                g_values = mm_tn(chances.astype(BF16), go)
                g_chances = mm_nt(go, values)
                inner = jnp.sum(chances * g_chances, axis=-1, keepdims=True)
                g_scores = jnp.where(allowed, chances * (g_chances - inner), 0.0).astype(BF16)
                g_queries = join_halves(mm(g_scores, keys)) * HEAD_DIM ** (-0.5)
                g_keys = mm_tn(g_scores, queries) * HEAD_DIM ** (-0.5)
                for part, value in enumerate((g_queries, g_keys, g_values)):
                    low = part * feature + start
                    gt_v[layer, :, low : low + PAIR] = value.astype(BF16)
            put(layer, 3, "gt", gt_v).start()
            small_v[layer, 2:3, :] = column_sum(gt_v[layer, :, :feature])
            small_v[layer, 3:4, :] = column_sum(gt_v[layer, :, 2 * feature :])
            weight_copy(layer, 3).wait()
            ga = mm_nt(gt_v[layer], wj_v[layer])
            saved_copy(layer, 3).wait()
            normed, scale = norm_parts(h_v[layer])
            small_v[layer, 0:1, :] = column_sum(ga * normed)
            small_v[layer, 1:2, :] = column_sum(ga)
            grad_v[...] = grad_v[...] + norm_back(normed, scale, vecs_v[layer, 0:1, :], ga)
            put(layer, 4, "small", small_v).start()
        out = pltpu.make_async_copy(grad_v, sent, in_sem.at[0])
        out.start()

        @pl.when(first == 1)
        def _():
            final = pltpu.make_async_copy(grad_v, stash["r"].at[slot], in_sem.at[1])
            final.start()
            final.wait()

        for layer in range(LAYERS):
            for index, (name, value_ref) in enumerate(
                (
                    ("gw", gw_v),
                    ("gu", gu_v),
                    ("gz", gz_v),
                    ("gt", gt_v),
                    ("small", small_v),
                )
            ):
                put(layer, index, name, value_ref).wait()
        out.wait()


def backward_step(branch_scale, flags, seeds, arrived, allowed, weights, vecs, saved, stash):
    length, feature = arrived.shape
    wj, wo, we, wc = weights
    hidden = we.shape[-1]
    scratch = [
        pltpu.VMEM(wj.shape, BF16),
        pltpu.VMEM(wo.shape, BF16),
        pltpu.VMEM(we.shape, BF16),
        pltpu.VMEM(wc.shape, BF16),
        pltpu.VMEM(vecs.shape, F32),
        pltpu.VMEM((length, length), F32),
        pltpu.VMEM((LAYERS, length, feature), F32),
        pltpu.VMEM((LAYERS, length, feature), F32),
        pltpu.VMEM((LAYERS, length, 3 * feature), BF16),
        pltpu.VMEM((LAYERS, length, hidden), BF16),
        pltpu.VMEM((length, feature), F32),
        pltpu.VMEM((LAYERS, length, feature), BF16),
        pltpu.VMEM((LAYERS, length, hidden), BF16),
        pltpu.VMEM((LAYERS, length, feature), BF16),
        pltpu.VMEM((length, feature), BF16),
        pltpu.VMEM((LAYERS, length, 3 * feature), BF16),
        pltpu.VMEM((LAYERS, 16, feature), F32),
        pltpu.SemaphoreType.DMA((LAYERS, 4)),
        pltpu.SemaphoreType.DMA((3,)),
        pltpu.SemaphoreType.DMA((LAYERS, 4)),
        pltpu.SemaphoreType.DMA((LAYERS, 5)),
    ]
    leading = 4 + 5 + len(saved)
    outs = pl.pallas_call(
        partial(backward_kernel, branch_scale),
        out_shape=tuple(jax.ShapeDtypeStruct(s.shape, s.dtype) for s in stash)
        + (jax.ShapeDtypeStruct((length, feature), F32),),
        in_specs=[SMEM] + [ANY] * (leading - 1 + len(stash)),
        out_specs=tuple([ANY] * (len(stash) + 1)),
        scratch_shapes=scratch,
        input_output_aliases={leading + i: i for i in range(len(stash))},
        compiler_params=pltpu.CompilerParams(vmem_limit_bytes=56 * 1024 * 1024),
        cost_estimate=pl.CostEstimate(
            flops=2 * length * sum(w.size for w in weights),
            bytes_accessed=2 * sum(w.size for w in weights),
            transcendentals=0,
        ),
        name="backward_step",
    )(flags, seeds, arrived, allowed, wj, wo, we, wc, vecs, *saved, *stash)
    return outs[:-1], outs[-1]


def empty_arrays(shapes):
    return pl.pallas_call(
        lambda *refs: None,
        out_shape=tuple(shapes),
        out_specs=tuple([ANY] * len(shapes)),
        name="empty_arrays",
    )()


def body(
    tokens,
    cotangent,
    document_lengths,
    valid_counts,
    first_gain,
    first_shift,
    joint_weight,
    query_value_offsets,
    output_weight,
    output_bias,
    second_gain,
    second_shift,
    expand_weight,
    expand_bias,
    contract_weight,
    contract_bias,
):
    sections = lax.axis_size("section")
    replicas = lax.axis_size("dp")
    section = lax.axis_index("section")
    replica = lax.axis_index("dp")
    near = 2 if replicas % 2 == 0 else 1
    far = replicas // near
    group, member = replica // near, replica % near
    micro_count, row_count, length, feature = tokens.shape
    hidden = expand_weight.shape[-1]
    own = micro_count * row_count
    rows = own * far
    branch_scale = (LAYERS * sections) ** (-0.5)
    first, last = section == 0, section == sections - 1
    positions = jnp.arange(length, dtype=jnp.int32)

    lengths = document_lengths.reshape(own, -1)
    live = (positions[None] < valid_counts.reshape(own, 1)).astype(F32)
    edge_own = jnp.where(
        first,
        tokens.reshape(own, length, feature).astype(F32),
        cotangent.reshape(own, length, feature).astype(F32) * live[:, :, None],
    )
    edges, all_lengths = [edge_own], [lengths]
    for shift in range(1, far):
        pairs = [
            (((g + shift) % far) * near + m, g * near + m) for g in range(far) for m in range(near)
        ]
        ends = sorted({0, sections - 1})
        all_lengths.append(lax.ppermute(lengths, "dp", pairs))
        edges.append(
            lax.ppermute(
                edge_own,
                ("section", "dp"),
                [(e * replicas + a, e * replicas + b) for e in ends for a, b in pairs],
            )
        )
    edge = jnp.concatenate(edges, axis=0)
    document_ends = jnp.cumsum(jnp.concatenate(all_lengths, axis=0), axis=-1)
    segment = jnp.sum(
        (positions[None, :, None] >= document_ends[:, None, :]).astype(jnp.int32), axis=-1
    )
    causal = positions[:, None] >= positions[None, :]
    allowed = ((segment[:, :, None] == segment[:, None, :]) & causal[None]).astype(F32)

    wide = [
        v.astype(F32)
        for v in (first_gain, first_shift, output_bias, second_gain, second_shift, contract_bias)
    ]
    blank = jnp.zeros_like(wide[0])
    vecs = jnp.stack(wide + [blank, blank], axis=1)
    offsets = query_value_offsets.astype(F32)
    bj = jnp.concatenate([offsets[:, :feature], blank, offsets[:, feature:]], axis=1)[:, None]
    be = expand_bias.astype(F32)[:, None]
    weights = (joint_weight, output_weight, expand_weight, contract_weight)

    def saved(width, dtype):
        return jax.ShapeDtypeStruct((LAYERS, rows, length, width), dtype)

    edge_shape = jax.ShapeDtypeStruct((rows, length, feature), F32)
    row_shape = jax.ShapeDtypeStruct((length, feature), F32)
    forward_shapes = (
        saved(feature, F32),
        saved(feature, F32),
        saved(feature, BF16),
        saved(3 * feature, BF16),
        saved(feature, BF16),
        saved(feature, BF16),
        saved(hidden, BF16),
        saved(hidden, BF16),
        edge_shape,
    )
    backward_shapes = (
        saved(feature, BF16),
        saved(hidden, BF16),
        saved(feature, BF16),
        saved(3 * feature, BF16),
        jax.ShapeDtypeStruct((LAYERS, rows, 16, feature), F32),
        edge_shape,
    )
    made = empty_arrays(forward_shapes + backward_shapes + (row_shape, row_shape))
    forward_stash = made[: len(forward_shapes)]
    backward_stash = made[len(forward_shapes) : -2]
    ticks = rows + 2 * (sections - 1)
    onward = [(i, i + 1) for i in range(sections - 1)]
    back = [(i + 1, i) for i in range(sections - 1)]

    def flags_of(row):
        active = (row >= 0) & (row < rows)
        return jnp.stack(
            [
                active.astype(jnp.int32),
                jnp.clip(row, 0, rows - 1),
                first.astype(jnp.int32),
                last.astype(jnp.int32),
            ]
        )

    def forward_tick(tick, carry):
        stash, sent, arrived = carry
        arriving = lax.ppermute(sent, "section", onward)
        flags = flags_of(tick - 2 * section)
        stash, out = forward_step(
            branch_scale, flags, edge, arrived, allowed, weights, (vecs, bj, be), stash
        )
        return stash, out, arriving

    forward_stash, _, _ = lax.fori_loop(
        0, ticks, forward_tick, (forward_stash, made[-2], made[-1])
    )
    sh, sg, sa, st, so, sc, sm, sd, final_rows = forward_stash

    def backward_tick(tick, carry):
        stash, sent, arrived = carry
        arriving = lax.ppermute(sent, "section", back)
        flags = flags_of(tick - 2 * (sections - 1 - section))
        stash, out = backward_step(
            branch_scale, flags, edge, arrived, allowed, weights, vecs, (sh, sg, st, sd), stash
        )
        return stash, out, arriving

    backward_stash, _, _ = lax.fori_loop(
        0, ticks, backward_tick, (backward_stash, made[-2], made[-1])
    )
    gw, gu, gz, gt, small, first_rows = backward_stash

    def near_sum(parts):
        mine = parts[0]
        for shift in range(1, near):
            pairs = [
                (g * near + m, g * near + (m + shift) % near)
                for g in range(far)
                for m in range(near)
            ]
            mine = mine + lax.ppermute(parts[shift], "dp", pairs)
        return mine

    def weight_gradient(left, right):
        width = left.shape[-1]
        left = left.reshape(LAYERS, rows * length, width)
        right = right.reshape(LAYERS, rows * length, right.shape[-1])
        left = lax.dynamic_slice_in_dim(left, group * (width // far), width // far, axis=2)
        product = jnp.einsum("lrd,lre->lde", left, right, preferred_element_type=F32)
        share = width // replicas
        return near_sum(
            [
                lax.dynamic_slice_in_dim(
                    product, ((member + shift) % near) * share, share, axis=1
                )
                for shift in range(near)
            ]
        )

    contract_gradient = weight_gradient(sm, gw)
    expand_gradient = weight_gradient(sc, gu)
    joint_gradient = weight_gradient(sa, gt)
    output_gradient = weight_gradient(so, gz)

    sums = jnp.sum(small, axis=1)
    vectors = [
        sums[:, 0],
        sums[:, 1],
        sums[:, 2:4].reshape(LAYERS, 2 * feature),
        sums[:, 6],
        sums[:, 4],
        sums[:, 5],
        sums[:, 8 : 8 + hidden // feature].reshape(LAYERS, hidden),
        sums[:, 7],
    ]
    packed = jnp.concatenate([v.reshape(LAYERS, replicas, -1) for v in vectors], axis=2)
    shared = near_sum(
        [
            lax.dynamic_index_in_dim(
                packed, group * near + (member + shift) % near, axis=1, keepdims=False
            )
            for shift in range(near)
        ]
    )
    pieces, at = [], 0
    for v in vectors:
        share = v.shape[1] // replicas
        pieces.append(shared[:, at : at + share])
        at += share

    share = feature // sections
    from_first = first_rows[:own].reshape(own, length, feature)
    from_last = final_rows[:own].reshape(own, length, feature)

    def columns(block, index):
        return block[:, :, index * share : (index + 1) * share]

    received = []
    for step in range(1, sections):
        payload = jnp.where(first, columns(from_first, step), columns(from_last, step - 1))
        received.append(
            lax.ppermute(payload, "section", [(0, step), (sections - 1, step - 1)])
        )
    gradient_slices = jnp.stack([columns(from_first, 0)] + received)
    final_slices = jnp.stack(received + [columns(from_last, sections - 1)])
    out_shape = (micro_count, row_count, length, share)
    input_gradient = lax.dynamic_index_in_dim(gradient_slices, section, keepdims=False)
    final_hidden = lax.dynamic_index_in_dim(final_slices, section, keepdims=False)
    return (
        final_hidden.reshape(out_shape),
        input_gradient.reshape(out_shape),
        pieces[0],
        pieces[1],
        joint_gradient,
        pieces[2],
        output_gradient,
        pieces[3],
        pieces[4],
        pieces[5],
        expand_gradient,
        pieces[6],
        contract_gradient,
        pieces[7],
    )


def solution(mesh):
    return jax.shard_map(
        body,
        mesh=mesh,
        in_specs=(
            P(None, "dp", None, None),
            P(None, "dp", None, None),
            P(None, "dp", None),
            P(None, "dp"),
            P("section", None),
            P("section", None),
            P("section", None, None),
            P("section", None),
            P("section", None, None),
            P("section", None),
            P("section", None),
            P("section", None),
            P("section", None, None),
            P("section", None),
            P("section", None, None),
            P("section", None),
        ),
        out_specs=(
            P(None, "dp", None, "section"),
            P(None, "dp", None, "section"),
            P("section", "dp"),
            P("section", "dp"),
            P("section", "dp", None),
            P("section", "dp"),
            P("section", "dp", None),
            P("section", "dp"),
            P("section", "dp"),
            P("section", "dp"),
            P("section", "dp", None),
            P("section", "dp"),
            P("section", "dp", None),
            P("section", "dp"),
        ),
        check_vma=False,
    )
```

```python
from functools import partial

import jax
import jax.numpy as jnp
from jax import lax
from jax.experimental import pallas as pl
from jax.experimental.pallas import tpu as pltpu
from jax.sharding import PartitionSpec as P

HEAD_DIM = 64
LAYERS = 2
PAIR = 2 * HEAD_DIM
SCOPED = 10368 * 1024
EPS = 1e-05
BF16 = jnp.bfloat16
F32 = jnp.float32
ANY = pl.BlockSpec(memory_space=pl.ANY)
VMEM = pl.BlockSpec(memory_space=pltpu.VMEM)
HBM = pl.BlockSpec(memory_space=pltpu.HBM)
UNROLL = 22
SMEM = pl.BlockSpec(memory_space=pltpu.SMEM)
TANH_SCALE = 0.7978845608028654


def mm(left, right):
    return lax.dot_general(left, right, (((1,), (0,)), ((), ())), preferred_element_type=F32)


def mm_nt(left, right):
    return lax.dot_general(left, right, (((1,), (1,)), ((), ())), preferred_element_type=F32)


def mm_tn(left, right):
    return lax.dot_general(left, right, (((0,), (0,)), ((), ())), preferred_element_type=F32)


def norm_parts(values):
    center = jnp.mean(values, axis=-1, keepdims=True)
    centered = values - center
    scale = lax.rsqrt(jnp.mean(centered * centered, axis=-1, keepdims=True) + EPS)
    return centered * scale, scale


def norm_back(normed, scale, gain, gradient):
    weighted = gradient * gain
    mean_weighted = jnp.mean(weighted, axis=-1, keepdims=True)
    mean_product = jnp.mean(weighted * normed, axis=-1, keepdims=True)
    return scale * (weighted - mean_weighted - normed * mean_product)


def stack_halves(block):
    low_lanes = lax.broadcasted_iota(jnp.int32, block.shape, 1) < HEAD_DIM
    zero = jnp.zeros_like(block)
    return jnp.concatenate(
        [jnp.where(low_lanes, block, zero), jnp.where(low_lanes, zero, block)], axis=0
    )


def join_halves(stacked):
    length = stacked.shape[0] // 2
    low_lanes = lax.broadcasted_iota(jnp.int32, (length, PAIR), 1) < HEAD_DIM
    return jnp.where(low_lanes, stacked[:length], stacked[length:])


def pair_probabilities(queries, keys, allowed):
    scores = mm_nt(queries, keys) * HEAD_DIM ** (-0.5)
    scores = jnp.where(allowed, scores, -1e30)
    powers = jnp.exp(scores - jnp.max(scores, axis=-1, keepdims=True))
    return powers / jnp.sum(powers, axis=-1, keepdims=True)


def column_sum(values):
    return jnp.sum(values.astype(F32), axis=0, keepdims=True)


def weight_blocks(weights):
    width = weights[1].shape[-1]
    return [
        (index, row, column)
        for index, weight in enumerate(weights)
        for row in range(0, weight.shape[1], width)
        for column in range(0, weight.shape[2], width)
    ]


def load_kernel(blocks, width, *refs):
    weights, targets, sems = refs[:4], refs[4:-1], refs[-1]
    copies = [
        pltpu.make_async_copy(
            weights[index].at[:, row : row + width, column : column + width],
            target,
            sems.at[at],
        )
        for at, ((index, row, column), target) in enumerate(zip(blocks, targets))
    ]
    for copy in copies:
        copy.start()
    for copy in copies:
        copy.wait()


def load_weights(weights):
    width = weights[1].shape[-1]
    blocks = weight_blocks(weights)
    return pl.pallas_call(
        partial(load_kernel, blocks, width),
        out_shape=tuple(pltpu.VMEM((LAYERS, width, width), BF16) for _ in blocks),
        in_specs=[ANY] * 4,
        out_specs=tuple([VMEM] * len(blocks)),
        scratch_shapes=[pltpu.SemaphoreType.DMA((len(blocks),))],
        compiler_params=pltpu.CompilerParams(vmem_limit_bytes=SCOPED),
        name="load_weights",
    )(*map(in_hbm, weights))


def in_hbm(value):
    return pltpu.with_memory_space_constraint(value, pltpu.HBM)


def layer_loop(body):
    lax.fori_loop(0, LAYERS, lambda index, carry: (body(index), carry)[1], 0)


def forward_kernel(branch_scale, joint_count, hidden_count, tick, tokens, arrived, allowed_rows, *refs):
    weight_count = joint_count + 1 + 2 * hidden_count
    wj = refs[:joint_count]
    wo = refs[joint_count]
    we = refs[joint_count + 1 : joint_count + 1 + hidden_count]
    wc = refs[joint_count + 1 + hidden_count : weight_count]
    vecs, bj, be = refs[weight_count : weight_count + 3]
    refs = refs[weight_count + 3 :]
    names = ("h", "g", "a", "t", "o", "c", "m", "d", "f")
    stash = dict(zip(names, refs[9:18]))
    sent, next_tick = refs[18:20]
    h_v, g_v, a_v, t_v, o_v, c_v, m_v, d_v, in_sem, out_sem = refs[20:]
    next_tick[0] = tick[0] + 1
    section = lax.axis_index("section")
    last = section == lax.axis_size("section") - 1
    feature = tokens.shape[-1]
    rows = allowed_rows.shape[0]
    row_index = tick[0] - 2 * section

    @pl.when((row_index >= 0) & (row_index < rows))
    def _():
        slot = jnp.clip(row_index, 0, rows - 1)

        @pl.when(section == 0)
        def _():
            pltpu.make_async_copy(tokens.at[lax.rem(slot, tokens.shape[0])], h_v.at[0], in_sem.at[0]).start()

        @pl.when(section > 0)
        def _():
            pltpu.make_async_copy(arrived, h_v.at[0], in_sem.at[0]).start()

        def put(layer, index, name, value_ref):
            return pltpu.make_async_copy(
                value_ref.at[layer], stash[name].at[layer, slot], out_sem.at[layer, index]
            )

        allowed = jnp.concatenate([allowed_rows[slot], allowed_rows[slot]], axis=0) > 0.5
        pltpu.make_async_copy(arrived, h_v.at[0], in_sem.at[0]).wait()

        def one_layer(layer):
            put(layer, 0, "h", h_v).start()
            row = h_v[layer]
            normed, _ = norm_parts(row)
            a_low = (normed * vecs[layer, 0:1, :] + vecs[layer, 1:2, :]).astype(BF16)
            a_v[layer] = a_low
            put(layer, 2, "a", a_v).start()
            for index in range(joint_count):
                span = slice(index * feature, (index + 1) * feature)
                t_v[layer, :, span] = (
                    mm(a_low, wj[index][layer]) + bj[layer, :, span]
                ).astype(BF16)
            put(layer, 3, "t", t_v).start()
            for start in range(0, feature, PAIR):
                queries = stack_halves(t_v[layer, :, start : start + PAIR])
                keys = t_v[layer, :, feature + start : feature + start + PAIR]
                values = t_v[layer, :, 2 * feature + start : 2 * feature + start + PAIR]
                chances = pair_probabilities(queries, keys, allowed).astype(BF16)
                o_v[layer, :, start : start + PAIR] = join_halves(mm(chances, values)).astype(BF16)
            put(layer, 4, "o", o_v).start()
            mixed = row + branch_scale * (mm(o_v[layer], wo[layer]) + vecs[layer, 2:3, :])
            g_v[layer] = mixed
            put(layer, 1, "g", g_v).start()
            normed, _ = norm_parts(mixed)
            c_low = (normed * vecs[layer, 3:4, :] + vecs[layer, 4:5, :]).astype(BF16)
            c_v[layer] = c_low
            put(layer, 5, "c", c_v).start()
            for index in range(hidden_count):
                span = slice(index * feature, (index + 1) * feature)
                u = mm(c_low, we[index][layer]) + be[layer, :, span]
                square = u * u
                th = jnp.tanh(TANH_SCALE * (u + 0.044715 * (square * u)))
                half = 0.5 * (1.0 + th)
                m_v[layer, :, span] = (u * half).astype(BF16)
                slope = half + 0.5 * u * (1.0 - th * th) * (
                    TANH_SCALE * (1.0 + 3.0 * 0.044715 * square)
                )
                d_v[layer, :, span] = slope.astype(BF16)
            put(layer, 6, "m", m_v).start()
            put(layer, 7, "d", d_v).start()
            z = vecs[layer, 5:6, :]
            for index in range(hidden_count):
                span = slice(index * feature, (index + 1) * feature)
                z = z + mm(m_v[layer, :, span], wc[index][layer])
            h_v[layer + 1] = mixed + branch_scale * z

        layer_loop(one_layer)
        sent[...] = h_v[LAYERS]

        @pl.when(last)
        def _():
            final = pltpu.make_async_copy(h_v.at[LAYERS], stash["f"].at[slot], in_sem.at[1])
            final.start()
            final.wait()

        for layer in range(LAYERS):
            for index, (name, value_ref) in enumerate(
                (
                    ("h", h_v),
                    ("g", g_v),
                    ("a", a_v),
                    ("t", t_v),
                    ("o", o_v),
                    ("c", c_v),
                    ("m", m_v),
                    ("d", d_v),
                )
            ):
                put(layer, index, name, value_ref).wait()


def counts_of(weights, feature):
    hidden_count = (len(weights) - 4) // 2
    return 3, hidden_count


def cost_of(length, weights):
    return pl.CostEstimate(
        flops=2 * length * sum(w.size for w in weights),
        bytes_accessed=2 * sum(w.size for w in weights),
        transcendentals=0,
    )


def forward_step(branch_scale, tick, tokens, arrived, allowed, weights, vectors, stash):
    length, feature = arrived.shape
    joint_count, hidden_count = counts_of(weights, feature)
    hidden = hidden_count * feature
    weights = tuple(pltpu.with_memory_space_constraint(w, pltpu.VMEM) for w in weights)
    scratch = [
        pltpu.VMEM((LAYERS + 1, length, feature), F32),
        pltpu.VMEM((LAYERS, length, feature), F32),
        pltpu.VMEM((LAYERS, length, feature), BF16),
        pltpu.VMEM((LAYERS, length, 3 * feature), BF16),
        pltpu.VMEM((LAYERS, length, feature), BF16),
        pltpu.VMEM((LAYERS, length, feature), BF16),
        pltpu.VMEM((LAYERS, length, hidden), BF16),
        pltpu.VMEM((LAYERS, length, hidden), BF16),
        pltpu.SemaphoreType.DMA((2,)),
        pltpu.SemaphoreType.DMA((LAYERS, 8)),
    ]
    leading = 4 + len(weights) + len(vectors)
    outs = pl.pallas_call(
        partial(forward_kernel, branch_scale, joint_count, hidden_count),
        out_shape=tuple(pltpu.HBM(s.shape, s.dtype) for s in stash)
        + (pltpu.VMEM((length, feature), F32), jax.ShapeDtypeStruct((1,), jnp.int32)),
        in_specs=[SMEM, ANY, ANY]
        + [VMEM] * (1 + len(weights) + len(vectors))
        + [HBM] * len(stash),
        out_specs=tuple([HBM] * len(stash) + [VMEM, SMEM]),
        scratch_shapes=scratch,
        input_output_aliases={leading + i: i for i in range(len(stash))},
        compiler_params=pltpu.CompilerParams(vmem_limit_bytes=SCOPED),
        cost_estimate=cost_of(length, weights),
        name="forward_step",
    )(tick, in_hbm(tokens), arrived, allowed, *weights, *vectors, *stash)
    return outs[:-2], outs[-2], outs[-1]


def backward_kernel(branch_scale, joint_count, hidden_count, tick, seeds, arrived, allowed_rows, *refs):
    weight_count = joint_count + 1 + 2 * hidden_count
    wj = refs[:joint_count]
    wo = refs[joint_count]
    we = refs[joint_count + 1 : joint_count + 1 + hidden_count]
    wc = refs[joint_count + 1 + hidden_count : weight_count]
    vecs, sh, sg, st, sd = refs[weight_count : weight_count + 5]
    refs = refs[weight_count + 5 :]
    names = ("gw", "gu", "gz", "gt", "small", "r")
    stash = dict(zip(names, refs[6:12]))
    sent, next_tick = refs[12:14]
    (
        h_v,
        g_v,
        t_v,
        d_v,
        grad_v,
        gw_v,
        gu_v,
        gz_v,
        go_v,
        gt_v,
        small_v,
        in_sem,
        s_sem,
        out_sem,
    ) = refs[14:]
    next_tick[0] = tick[0] + 1
    section = lax.axis_index("section")
    sections = lax.axis_size("section")
    _, length, feature = seeds.shape
    rows = allowed_rows.shape[0]
    row_index = tick[0] - 2 * (sections - 1 - section)

    @pl.when((row_index >= 0) & (row_index < rows))
    def _():
        slot = jnp.clip(row_index, 0, rows - 1)

        @pl.when(section == sections - 1)
        def _():
            pltpu.make_async_copy(seeds.at[lax.rem(slot, seeds.shape[0])], grad_v, in_sem.at[0]).start()

        @pl.when(section < sections - 1)
        def _():
            pltpu.make_async_copy(arrived, grad_v, in_sem.at[0]).start()

        saved = ((sd, d_v), (sg, g_v), (st, t_v), (sh, h_v))

        def saved_copy(layer, index):
            source, target = saved[index]
            return pltpu.make_async_copy(
                source.at[layer, slot], target.at[layer], s_sem.at[layer, index]
            )

        for layer in reversed(range(LAYERS)):
            for index in range(4):
                saved_copy(layer, index).start()

        def put(layer, index, name, value_ref):
            return pltpu.make_async_copy(
                value_ref.at[layer], stash[name].at[layer, slot], out_sem.at[layer, index]
            )

        allowed = jnp.concatenate([allowed_rows[slot], allowed_rows[slot]], axis=0) > 0.5
        pltpu.make_async_copy(arrived, grad_v, in_sem.at[0]).wait()

        def one_layer(turn):
            layer = LAYERS - 1 - turn
            gw = (branch_scale * grad_v[...]).astype(BF16)
            gw_v[layer] = gw
            put(layer, 0, "gw", gw_v).start()
            small_v[layer, 7:8, :] = column_sum(gw)
            saved_copy(layer, 0).wait()
            gc = jnp.zeros((length, feature), F32)
            for index in range(hidden_count):
                span = slice(index * feature, (index + 1) * feature)
                gu = (d_v[layer, :, span].astype(F32) * mm_nt(gw, wc[index][layer])).astype(BF16)
                gu_v[layer, :, span] = gu
                small_v[layer, 8 + index : 9 + index, :] = column_sum(gu)
            put(layer, 1, "gu", gu_v).start()
            for index in range(hidden_count):
                span = slice(index * feature, (index + 1) * feature)
                gc = gc + mm_nt(gu_v[layer, :, span], we[index][layer])
            saved_copy(layer, 1).wait()
            normed, scale = norm_parts(g_v[layer])
            small_v[layer, 4:5, :] = column_sum(gc * normed)
            small_v[layer, 5:6, :] = column_sum(gc)
            gg = grad_v[...] + norm_back(normed, scale, vecs[layer, 3:4, :], gc)
            grad_v[...] = gg
            gz = (branch_scale * gg).astype(BF16)
            gz_v[layer] = gz
            put(layer, 2, "gz", gz_v).start()
            small_v[layer, 6:7, :] = column_sum(gz)
            go_v[...] = mm_nt(gz, wo[layer]).astype(BF16)
            saved_copy(layer, 2).wait()
            for start in range(0, feature, PAIR):
                queries = stack_halves(t_v[layer, :, start : start + PAIR])
                keys = t_v[layer, :, feature + start : feature + start + PAIR]
                values = t_v[layer, :, 2 * feature + start : 2 * feature + start + PAIR]
                go = stack_halves(go_v[:, start : start + PAIR])
                chances = pair_probabilities(queries, keys, allowed)
                g_values = mm_tn(chances.astype(BF16), go)
                g_chances = mm_nt(go, values)
                inner = jnp.sum(chances * g_chances, axis=-1, keepdims=True)
                g_scores = jnp.where(allowed, chances * (g_chances - inner), 0.0).astype(BF16)
                g_queries = join_halves(mm(g_scores, keys)) * HEAD_DIM ** (-0.5)
                g_keys = mm_tn(g_scores, queries) * HEAD_DIM ** (-0.5)
                for part, value in enumerate((g_queries, g_keys, g_values)):
                    low = part * feature + start
                    gt_v[layer, :, low : low + PAIR] = value.astype(BF16)
            put(layer, 3, "gt", gt_v).start()
            small_v[layer, 2:3, :] = column_sum(gt_v[layer, :, :feature])
            small_v[layer, 3:4, :] = column_sum(gt_v[layer, :, 2 * feature :])
            ga = jnp.zeros((length, feature), F32)
            for index in range(joint_count):
                span = slice(index * feature, (index + 1) * feature)
                ga = ga + mm_nt(gt_v[layer, :, span], wj[index][layer])
            saved_copy(layer, 3).wait()
            normed, scale = norm_parts(h_v[layer])
            small_v[layer, 0:1, :] = column_sum(ga * normed)
            small_v[layer, 1:2, :] = column_sum(ga)
            grad_v[...] = grad_v[...] + norm_back(normed, scale, vecs[layer, 0:1, :], ga)
            put(layer, 4, "small", small_v).start()

        layer_loop(one_layer)
        sent[...] = grad_v[...]

        @pl.when(section == 0)
        def _():
            final = pltpu.make_async_copy(grad_v, stash["r"].at[slot], in_sem.at[1])
            final.start()
            final.wait()

        for layer in range(LAYERS):
            for index, (name, value_ref) in enumerate(
                (
                    ("gw", gw_v),
                    ("gu", gu_v),
                    ("gz", gz_v),
                    ("gt", gt_v),
                    ("small", small_v),
                )
            ):
                put(layer, index, name, value_ref).wait()


def backward_step(branch_scale, tick, seeds, arrived, allowed, weights, vecs, saved, stash):
    length, feature = arrived.shape
    joint_count, hidden_count = counts_of(weights, feature)
    hidden = hidden_count * feature
    weights = tuple(pltpu.with_memory_space_constraint(w, pltpu.VMEM) for w in weights)
    scratch = [
        pltpu.VMEM((LAYERS, length, feature), F32),
        pltpu.VMEM((LAYERS, length, feature), F32),
        pltpu.VMEM((LAYERS, length, 3 * feature), BF16),
        pltpu.VMEM((LAYERS, length, hidden), BF16),
        pltpu.VMEM((length, feature), F32),
        pltpu.VMEM((LAYERS, length, feature), BF16),
        pltpu.VMEM((LAYERS, length, hidden), BF16),
        pltpu.VMEM((LAYERS, length, feature), BF16),
        pltpu.VMEM((length, feature), BF16),
        pltpu.VMEM((LAYERS, length, 3 * feature), BF16),
        pltpu.VMEM((LAYERS, 16, feature), F32),
        pltpu.SemaphoreType.DMA((2,)),
        pltpu.SemaphoreType.DMA((LAYERS, 4)),
        pltpu.SemaphoreType.DMA((LAYERS, 5)),
    ]
    leading = 5 + len(weights) + len(saved)
    outs = pl.pallas_call(
        partial(backward_kernel, branch_scale, joint_count, hidden_count),
        out_shape=tuple(pltpu.HBM(s.shape, s.dtype) for s in stash)
        + (pltpu.VMEM((length, feature), F32), jax.ShapeDtypeStruct((1,), jnp.int32)),
        in_specs=[SMEM, ANY, ANY]
        + [VMEM] * (2 + len(weights))
        + [HBM] * (len(saved) + len(stash)),
        out_specs=tuple([HBM] * len(stash) + [VMEM, SMEM]),
        scratch_shapes=scratch,
        input_output_aliases={leading + i: i for i in range(len(stash))},
        compiler_params=pltpu.CompilerParams(vmem_limit_bytes=SCOPED),
        cost_estimate=cost_of(length, weights),
        name="backward_step",
    )(tick, in_hbm(seeds), arrived, allowed, *weights, vecs, *map(in_hbm, saved), *stash)
    return outs[:-2], outs[-2], outs[-1]


def empty_arrays(shapes):
    return pl.pallas_call(
        lambda *refs: None,
        out_shape=tuple(pltpu.HBM(s.shape, s.dtype) for s in shapes),
        out_specs=tuple([HBM] * len(shapes)),
        name="empty_arrays",
    )()


def body(
    tokens,
    cotangent,
    document_lengths,
    valid_counts,
    first_gain,
    first_shift,
    joint_weight,
    query_value_offsets,
    output_weight,
    output_bias,
    second_gain,
    second_shift,
    expand_weight,
    expand_bias,
    contract_weight,
    contract_bias,
):
    sections = lax.axis_size("section")
    replicas = lax.axis_size("dp")
    section = lax.axis_index("section")
    replica = lax.axis_index("dp")
    near = 2 if replicas % 2 == 0 else 1
    far = replicas // near
    group, member = replica // near, replica % near
    micro_count, row_count, length, feature = tokens.shape
    hidden = expand_weight.shape[-1]
    own = micro_count * row_count
    rows = own * far
    branch_scale = (LAYERS * sections) ** (-0.5)
    first, last = section == 0, section == sections - 1
    positions = jnp.arange(length, dtype=jnp.int32)

    lengths = document_lengths.reshape(own, -1)
    live = (positions[None] < valid_counts.reshape(own, 1)).astype(F32)
    edge_own = jnp.where(
        first,
        tokens.reshape(own, length, feature).astype(F32),
        cotangent.reshape(own, length, feature).astype(F32) * live[:, :, None],
    )
    edges, all_lengths = [edge_own], [lengths]
    for shift in range(1, far):
        pairs = [
            (((g + shift) % far) * near + m, g * near + m) for g in range(far) for m in range(near)
        ]
        ends = sorted({0, sections - 1})
        all_lengths.append(lax.ppermute(lengths, "dp", pairs))
        edges.append(
            lax.ppermute(
                edge_own,
                ("section", "dp"),
                [(e * replicas + a, e * replicas + b) for e in ends for a, b in pairs],
            )
        )
    document_ends = jnp.cumsum(jnp.concatenate(all_lengths, axis=0), axis=-1)
    segment = jnp.sum(
        (positions[None, :, None] >= document_ends[:, None, :]).astype(jnp.int32), axis=-1
    )
    causal = positions[:, None] >= positions[None, :]
    allowed = ((segment[:, :, None] == segment[:, None, :]) & causal[None]).astype(F32)

    wide = [
        v.astype(F32)
        for v in (first_gain, first_shift, output_bias, second_gain, second_shift, contract_bias)
    ]
    blank = jnp.zeros_like(wide[0])
    vecs = jnp.stack(wide + [blank, blank], axis=1)
    offsets = query_value_offsets.astype(F32)
    bj = jnp.concatenate([offsets[:, :feature], blank, offsets[:, feature:]], axis=1)[:, None]
    be = expand_bias.astype(F32)[:, None]
    weights = (joint_weight, output_weight, expand_weight, contract_weight)

    def saved(width, dtype):
        return jax.ShapeDtypeStruct((LAYERS, rows, length, width), dtype)

    edge_shape = jax.ShapeDtypeStruct((rows, length, feature), F32)
    row_shape = jax.ShapeDtypeStruct((length, feature), F32)
    forward_shapes = (
        saved(feature, F32),
        saved(feature, F32),
        saved(feature, BF16),
        saved(3 * feature, BF16),
        saved(feature, BF16),
        saved(feature, BF16),
        saved(hidden, BF16),
        saved(hidden, BF16),
        edge_shape,
    )
    backward_shapes = (
        saved(feature, BF16),
        saved(hidden, BF16),
        saved(feature, BF16),
        saved(3 * feature, BF16),
        jax.ShapeDtypeStruct((LAYERS, rows, 16, feature), F32),
        edge_shape,
    )
    made = empty_arrays(forward_shapes + backward_shapes + (row_shape, row_shape))
    forward_stash = made[: len(forward_shapes)]
    backward_stash = made[len(forward_shapes) : -2]
    ticks = rows + 2 * (sections - 1)
    onward = [(i, i + 1) for i in range(sections - 1)]
    back = [(i + 1, i) for i in range(sections - 1)]

    vectors = lax.optimization_barrier((vecs, bj, be))
    allowed = lax.optimization_barrier(allowed)
    loaded = load_weights(weights)
    chunk = min(ticks, UNROLL)
    rounds = -(-ticks // chunk)
    edge = jnp.concatenate(edges, axis=0) if rounds > 1 else None

    def run(step, pairs, stash):
        def turn(carry, source_of):
            stash, sent, arrived, tick = carry
            for index in range(chunk):
                arriving = lax.ppermute(sent, "section", pairs)
                stash, sent, tick = step(tick, source_of(index), arrived, stash)
                arrived = arriving
            return stash, sent, arrived, tick

        start = (stash, made[-2], made[-1], jnp.zeros((1,), jnp.int32))
        if rounds == 1:
            return turn(start, lambda index: edges[min(index, rows - 1) // own])[::3]
        return lax.fori_loop(0, rounds, lambda _, carry: turn(carry, lambda index: edge), start)[::3]

    forward_stash, walked = run(
        lambda tick, source, arrived, stash: forward_step(
            branch_scale, tick, source, arrived, allowed, loaded, vectors, stash
        ),
        onward,
        forward_stash,
    )
    sh, sg, sa, st, so, sc, sm, sd, final_rows = forward_stash

    backward_stash, _ = run(
        lambda tick, source, arrived, stash: backward_step(
            branch_scale, tick, source, arrived, allowed, loaded, vectors[0], (sh, sg, st, sd), stash
        ),
        back,
        backward_stash,
    )
    gw, gu, gz, gt, small, first_rows = backward_stash

    def near_sum(parts):
        mine = parts[0]
        for shift in range(1, near):
            pairs = [
                (g * near + m, g * near + (m + shift) % near)
                for g in range(far)
                for m in range(near)
            ]
            mine = mine + lax.ppermute(parts[shift], "dp", pairs)
        return mine

    def weight_gradient(left, right):
        width = left.shape[-1]
        left = left.reshape(LAYERS, rows * length, width)
        right = right.reshape(LAYERS, rows * length, right.shape[-1])
        left = lax.dynamic_slice_in_dim(left, group * (width // far), width // far, axis=2)
        product = jnp.einsum("lrd,lre->lde", left, right, preferred_element_type=F32)
        share = width // replicas
        return near_sum(
            [
                lax.dynamic_slice_in_dim(
                    product, ((member + shift) % near) * share, share, axis=1
                )
                for shift in range(near)
            ]
        )

    contract_gradient = weight_gradient(sm, gw)
    expand_gradient = weight_gradient(sc, gu)
    joint_gradient = weight_gradient(sa, gt)
    output_gradient = weight_gradient(so, gz)

    sums = jnp.sum(small, axis=1)
    vectors = [
        sums[:, 0],
        sums[:, 1],
        sums[:, 2:4].reshape(LAYERS, 2 * feature),
        sums[:, 6],
        sums[:, 4],
        sums[:, 5],
        sums[:, 8 : 8 + hidden // feature].reshape(LAYERS, hidden),
        sums[:, 7],
    ]
    packed = jnp.concatenate([v.reshape(LAYERS, replicas, -1) for v in vectors], axis=2)
    shared = near_sum(
        [
            lax.dynamic_index_in_dim(
                packed, group * near + (member + shift) % near, axis=1, keepdims=False
            )
            for shift in range(near)
        ]
    )
    pieces, at = [], 0
    for v in vectors:
        share = v.shape[1] // replicas
        pieces.append(shared[:, at : at + share])
        at += share

    share = feature // sections
    from_first = first_rows[:own].reshape(own, length, feature)
    from_last = final_rows[:own].reshape(own, length, feature)

    def columns(block, index):
        return block[:, :, index * share : (index + 1) * share]

    received = []
    for step in range(1, sections):
        payload = jnp.where(first, columns(from_first, step), columns(from_last, step - 1))
        received.append(
            lax.ppermute(payload, "section", [(0, step), (sections - 1, step - 1)])
        )
    gradient_slices = jnp.stack([columns(from_first, 0)] + received)
    final_slices = jnp.stack(received + [columns(from_last, sections - 1)])
    out_shape = (micro_count, row_count, length, share)
    input_gradient = lax.dynamic_index_in_dim(gradient_slices, section, keepdims=False)
    final_hidden = lax.dynamic_index_in_dim(final_slices, section, keepdims=False)
    return (
        final_hidden.reshape(out_shape),
        input_gradient.reshape(out_shape),
        pieces[0],
        pieces[1],
        joint_gradient,
        pieces[2],
        output_gradient,
        pieces[3],
        pieces[4],
        pieces[5],
        expand_gradient,
        pieces[6],
        contract_gradient,
        pieces[7],
    )


def solution(mesh):
    return jax.shard_map(
        body,
        mesh=mesh,
        in_specs=(
            P(None, "dp", None, None),
            P(None, "dp", None, None),
            P(None, "dp", None),
            P(None, "dp"),
            P("section", None),
            P("section", None),
            P("section", None, None),
            P("section", None),
            P("section", None, None),
            P("section", None),
            P("section", None),
            P("section", None),
            P("section", None, None),
            P("section", None),
            P("section", None, None),
            P("section", None),
        ),
        out_specs=(
            P(None, "dp", None, "section"),
            P(None, "dp", None, "section"),
            P("section", "dp"),
            P("section", "dp"),
            P("section", "dp", None),
            P("section", "dp"),
            P("section", "dp", None),
            P("section", "dp"),
            P("section", "dp"),
            P("section", "dp"),
            P("section", "dp", None),
            P("section", "dp"),
            P("section", "dp", None),
            P("section", "dp"),
        ),
        check_vma=False,
    )
```

```python
from functools import partial

import jax
import jax.numpy as jnp
from jax import lax
from jax.experimental import pallas as pl
from jax.experimental.pallas import tpu as pltpu
from jax.sharding import PartitionSpec as P

HEAD_DIM = 64
LAYERS = 2
PAIR = 2 * HEAD_DIM
SCOPED = 10368 * 1024
EPS = 1e-05
BF16 = jnp.bfloat16
F32 = jnp.float32
ANY = pl.BlockSpec(memory_space=pl.ANY)
VMEM = pl.BlockSpec(memory_space=pltpu.VMEM)
HBM = pl.BlockSpec(memory_space=pltpu.HBM)
UNROLL = 22
SMEM = pl.BlockSpec(memory_space=pltpu.SMEM)
TANH_SCALE = 0.7978845608028654


def mm(left, right):
    return lax.dot_general(left, right, (((1,), (0,)), ((), ())), preferred_element_type=F32)


def mm_nt(left, right):
    return lax.dot_general(left, right, (((1,), (1,)), ((), ())), preferred_element_type=F32)


def mm_tn(left, right):
    return lax.dot_general(left, right, (((0,), (0,)), ((), ())), preferred_element_type=F32)


def norm_parts(values):
    center = jnp.mean(values, axis=-1, keepdims=True)
    centered = values - center
    scale = lax.rsqrt(jnp.mean(centered * centered, axis=-1, keepdims=True) + EPS)
    return centered * scale, scale


def norm_back(normed, scale, gain, gradient):
    weighted = gradient * gain
    mean_weighted = jnp.mean(weighted, axis=-1, keepdims=True)
    mean_product = jnp.mean(weighted * normed, axis=-1, keepdims=True)
    return scale * (weighted - mean_weighted - normed * mean_product)


def stack_halves(block):
    low_lanes = lax.broadcasted_iota(jnp.int32, block.shape, 1) < HEAD_DIM
    zero = jnp.zeros_like(block)
    return jnp.concatenate(
        [jnp.where(low_lanes, block, zero), jnp.where(low_lanes, zero, block)], axis=0
    )


def join_halves(stacked):
    length = stacked.shape[0] // 2
    low_lanes = lax.broadcasted_iota(jnp.int32, (length, PAIR), 1) < HEAD_DIM
    return jnp.where(low_lanes, stacked[:length], stacked[length:])


def pair_probabilities(queries, keys, allowed):
    scores = mm_nt(queries, keys) * HEAD_DIM ** (-0.5)
    scores = jnp.where(allowed, scores, -1e30)
    powers = jnp.exp(scores - jnp.max(scores, axis=-1, keepdims=True))
    return powers / jnp.sum(powers, axis=-1, keepdims=True)


def column_sum(values):
    return jnp.sum(values.astype(F32), axis=0, keepdims=True)


def weight_blocks(weights):
    width = weights[1].shape[-1]
    return [
        (index, row, column)
        for index, weight in enumerate(weights)
        for row in range(0, weight.shape[1], width)
        for column in range(0, weight.shape[2], width)
    ]


def load_kernel(blocks, width, *refs):
    weights, targets, sems = refs[:4], refs[4:-1], refs[-1]
    copies = [
        pltpu.make_async_copy(
            weights[index].at[:, row : row + width, column : column + width],
            target,
            sems.at[at],
        )
        for at, ((index, row, column), target) in enumerate(zip(blocks, targets))
    ]
    for copy in copies:
        copy.start()
    for copy in copies:
        copy.wait()


def load_weights(weights):
    width = weights[1].shape[-1]
    blocks = weight_blocks(weights)
    return pl.pallas_call(
        partial(load_kernel, blocks, width),
        out_shape=tuple(pltpu.VMEM((LAYERS, width, width), BF16) for _ in blocks),
        in_specs=[ANY] * 4,
        out_specs=tuple([VMEM] * len(blocks)),
        scratch_shapes=[pltpu.SemaphoreType.DMA((len(blocks),))],
        compiler_params=pltpu.CompilerParams(vmem_limit_bytes=SCOPED),
        name="load_weights",
    )(*map(in_hbm, weights))


def in_hbm(value):
    return pltpu.with_memory_space_constraint(value, pltpu.HBM)


def layer_loop(body):
    lax.fori_loop(0, LAYERS, lambda index, carry: (body(index), carry)[1], 0)


def forward_kernel(branch_scale, joint_count, hidden_count, tick, tokens, arrived, allowed_rows, *refs):
    weight_count = joint_count + 1 + 2 * hidden_count
    wj = refs[:joint_count]
    wo = refs[joint_count]
    we = refs[joint_count + 1 : joint_count + 1 + hidden_count]
    wc = refs[joint_count + 1 + hidden_count : weight_count]
    vecs, bj, be = refs[weight_count : weight_count + 3]
    refs = refs[weight_count + 3 :]
    names = ("h", "g", "a", "t", "o", "c", "m", "d", "f")
    stash = dict(zip(names, refs[9:18]))
    sent, next_tick = refs[18:20]
    h_v, g_v, a_v, t_v, o_v, c_v, m_v, d_v, in_sem, out_sem = refs[20:]
    next_tick[0] = tick[0] + 1
    section = lax.axis_index("section")
    last = section == lax.axis_size("section") - 1
    feature = tokens.shape[-1]
    rows = allowed_rows.shape[0]
    row_index = tick[0] - 2 * section

    @pl.when((row_index >= 0) & (row_index < rows))
    def _():
        slot = jnp.clip(row_index, 0, rows - 1)

        @pl.when(section == 0)
        def _():
            pltpu.make_async_copy(tokens.at[lax.rem(slot, tokens.shape[0])], h_v.at[0], in_sem.at[0]).start()

        @pl.when(section > 0)
        def _():
            pltpu.make_async_copy(arrived, h_v.at[0], in_sem.at[0]).start()

        def put(layer, index, name, value_ref):
            return pltpu.make_async_copy(
                value_ref.at[layer], stash[name].at[layer, slot], out_sem.at[layer, index]
            )

        allowed = jnp.concatenate([allowed_rows[slot], allowed_rows[slot]], axis=0) > 0.5
        pltpu.make_async_copy(arrived, h_v.at[0], in_sem.at[0]).wait()

        def one_layer(layer):
            put(layer, 0, "h", h_v).start()
            row = h_v[layer]
            normed, _ = norm_parts(row)
            a_low = (normed * vecs[layer, 0:1, :] + vecs[layer, 1:2, :]).astype(BF16)
            a_v[layer] = a_low
            put(layer, 2, "a", a_v).start()
            for index in range(joint_count):
                span = slice(index * feature, (index + 1) * feature)
                t_v[layer, :, span] = (
                    mm(a_low, wj[index][layer]) + bj[layer, :, span]
                ).astype(BF16)
            put(layer, 3, "t", t_v).start()
            for start in range(0, feature, PAIR):
                queries = stack_halves(t_v[layer, :, start : start + PAIR])
                keys = t_v[layer, :, feature + start : feature + start + PAIR]
                values = t_v[layer, :, 2 * feature + start : 2 * feature + start + PAIR]
                chances = pair_probabilities(queries, keys, allowed).astype(BF16)
                o_v[layer, :, start : start + PAIR] = join_halves(mm(chances, values)).astype(BF16)
            put(layer, 4, "o", o_v).start()
            mixed = row + branch_scale * (mm(o_v[layer], wo[layer]) + vecs[layer, 2:3, :])
            g_v[layer] = mixed
            put(layer, 1, "g", g_v).start()
            normed, _ = norm_parts(mixed)
            c_low = (normed * vecs[layer, 3:4, :] + vecs[layer, 4:5, :]).astype(BF16)
            c_v[layer] = c_low
            put(layer, 5, "c", c_v).start()
            for index in range(hidden_count):
                span = slice(index * feature, (index + 1) * feature)
                u = mm(c_low, we[index][layer]) + be[layer, :, span]
                square = u * u
                th = jnp.tanh(TANH_SCALE * (u + 0.044715 * (square * u)))
                half = 0.5 * (1.0 + th)
                m_v[layer, :, span] = (u * half).astype(BF16)
                slope = half + 0.5 * u * (1.0 - th * th) * (
                    TANH_SCALE * (1.0 + 3.0 * 0.044715 * square)
                )
                d_v[layer, :, span] = slope.astype(BF16)
            put(layer, 6, "m", m_v).start()
            put(layer, 7, "d", d_v).start()
            z = vecs[layer, 5:6, :]
            for index in range(hidden_count):
                span = slice(index * feature, (index + 1) * feature)
                z = z + mm(m_v[layer, :, span], wc[index][layer])
            h_v[layer + 1] = mixed + branch_scale * z

        layer_loop(one_layer)
        sent[...] = h_v[LAYERS]

        @pl.when(last)
        def _():
            final = pltpu.make_async_copy(h_v.at[LAYERS], stash["f"].at[slot], in_sem.at[1])
            final.start()
            final.wait()

        for layer in range(LAYERS):
            for index, (name, value_ref) in enumerate(
                (
                    ("h", h_v),
                    ("g", g_v),
                    ("a", a_v),
                    ("t", t_v),
                    ("o", o_v),
                    ("c", c_v),
                    ("m", m_v),
                    ("d", d_v),
                )
            ):
                put(layer, index, name, value_ref).wait()


def counts_of(weights, feature):
    hidden_count = (len(weights) - 4) // 2
    return 3, hidden_count


def cost_of(length, weights):
    return pl.CostEstimate(
        flops=2 * length * sum(w.size for w in weights),
        bytes_accessed=2 * sum(w.size for w in weights),
        transcendentals=0,
    )


def forward_step(branch_scale, tick, tokens, arrived, allowed, weights, vectors, stash):
    length, feature = arrived.shape
    joint_count, hidden_count = counts_of(weights, feature)
    hidden = hidden_count * feature
    weights = tuple(pltpu.with_memory_space_constraint(w, pltpu.VMEM) for w in weights)
    scratch = [
        pltpu.VMEM((LAYERS + 1, length, feature), F32),
        pltpu.VMEM((LAYERS, length, feature), F32),
        pltpu.VMEM((LAYERS, length, feature), BF16),
        pltpu.VMEM((LAYERS, length, 3 * feature), BF16),
        pltpu.VMEM((LAYERS, length, feature), BF16),
        pltpu.VMEM((LAYERS, length, feature), BF16),
        pltpu.VMEM((LAYERS, length, hidden), BF16),
        pltpu.VMEM((LAYERS, length, hidden), BF16),
        pltpu.SemaphoreType.DMA((2,)),
        pltpu.SemaphoreType.DMA((LAYERS, 8)),
    ]
    leading = 4 + len(weights) + len(vectors)
    outs = pl.pallas_call(
        partial(forward_kernel, branch_scale, joint_count, hidden_count),
        out_shape=tuple(pltpu.HBM(s.shape, s.dtype) for s in stash)
        + (pltpu.VMEM((length, feature), F32), jax.ShapeDtypeStruct((1,), jnp.int32)),
        in_specs=[SMEM, ANY, ANY]
        + [VMEM] * (1 + len(weights) + len(vectors))
        + [HBM] * len(stash),
        out_specs=tuple([HBM] * len(stash) + [VMEM, SMEM]),
        scratch_shapes=scratch,
        input_output_aliases={leading + i: i for i in range(len(stash))},
        compiler_params=pltpu.CompilerParams(vmem_limit_bytes=SCOPED),
        cost_estimate=cost_of(length, weights),
        name="forward_step",
    )(tick, in_hbm(tokens), arrived, allowed, *weights, *vectors, *stash)
    return outs[:-2], outs[-2], outs[-1]


def backward_kernel(branch_scale, joint_count, hidden_count, tick, seeds, arrived, allowed_rows, *refs):
    weight_count = joint_count + 1 + 2 * hidden_count
    wj = refs[:joint_count]
    wo = refs[joint_count]
    we = refs[joint_count + 1 : joint_count + 1 + hidden_count]
    wc = refs[joint_count + 1 + hidden_count : weight_count]
    vecs, sh, sg, st, sd = refs[weight_count : weight_count + 5]
    refs = refs[weight_count + 5 :]
    names = ("gw", "gu", "gz", "gt", "small", "r")
    stash = dict(zip(names, refs[6:12]))
    sent, next_tick = refs[12:14]
    (
        h_v,
        g_v,
        t_v,
        d_v,
        grad_v,
        gw_v,
        gu_v,
        gz_v,
        go_v,
        gt_v,
        small_v,
        in_sem,
        s_sem,
        out_sem,
    ) = refs[14:]
    next_tick[0] = tick[0] + 1
    section = lax.axis_index("section")
    sections = lax.axis_size("section")
    _, length, feature = seeds.shape
    rows = allowed_rows.shape[0]
    row_index = tick[0] - 2 * (sections - 1 - section)

    @pl.when((row_index >= 0) & (row_index < rows))
    def _():
        slot = jnp.clip(row_index, 0, rows - 1)

        @pl.when(section == sections - 1)
        def _():
            pltpu.make_async_copy(seeds.at[lax.rem(slot, seeds.shape[0])], grad_v, in_sem.at[0]).start()

        @pl.when(section < sections - 1)
        def _():
            pltpu.make_async_copy(arrived, grad_v, in_sem.at[0]).start()

        saved = ((sd, d_v), (sg, g_v), (st, t_v), (sh, h_v))

        def saved_copy(layer, index):
            source, target = saved[index]
            return pltpu.make_async_copy(
                source.at[layer, slot], target.at[layer], s_sem.at[layer, index]
            )

        for layer in reversed(range(LAYERS)):
            for index in range(4):
                saved_copy(layer, index).start()

        def put(layer, index, name, value_ref):
            return pltpu.make_async_copy(
                value_ref.at[layer], stash[name].at[layer, slot], out_sem.at[layer, index]
            )

        allowed = jnp.concatenate([allowed_rows[slot], allowed_rows[slot]], axis=0) > 0.5
        pltpu.make_async_copy(arrived, grad_v, in_sem.at[0]).wait()

        def one_layer(turn):
            layer = LAYERS - 1 - turn
            gw = (branch_scale * grad_v[...]).astype(BF16)
            gw_v[layer] = gw
            put(layer, 0, "gw", gw_v).start()
            small_v[layer, 7:8, :] = column_sum(gw)
            saved_copy(layer, 0).wait()
            gc = jnp.zeros((length, feature), F32)
            for index in range(hidden_count):
                span = slice(index * feature, (index + 1) * feature)
                gu = (d_v[layer, :, span].astype(F32) * mm_nt(gw, wc[index][layer])).astype(BF16)
                gu_v[layer, :, span] = gu
                small_v[layer, 8 + index : 9 + index, :] = column_sum(gu)
            put(layer, 1, "gu", gu_v).start()
            for index in range(hidden_count):
                span = slice(index * feature, (index + 1) * feature)
                gc = gc + mm_nt(gu_v[layer, :, span], we[index][layer])
            saved_copy(layer, 1).wait()
            normed, scale = norm_parts(g_v[layer])
            small_v[layer, 4:5, :] = column_sum(gc * normed)
            small_v[layer, 5:6, :] = column_sum(gc)
            gg = grad_v[...] + norm_back(normed, scale, vecs[layer, 3:4, :], gc)
            grad_v[...] = gg
            gz = (branch_scale * gg).astype(BF16)
            gz_v[layer] = gz
            put(layer, 2, "gz", gz_v).start()
            small_v[layer, 6:7, :] = column_sum(gz)
            go_v[...] = mm_nt(gz, wo[layer]).astype(BF16)
            saved_copy(layer, 2).wait()
            for start in range(0, feature, PAIR):
                queries = stack_halves(t_v[layer, :, start : start + PAIR])
                keys = t_v[layer, :, feature + start : feature + start + PAIR]
                values = t_v[layer, :, 2 * feature + start : 2 * feature + start + PAIR]
                go = stack_halves(go_v[:, start : start + PAIR])
                chances = pair_probabilities(queries, keys, allowed)
                g_values = mm_tn(chances.astype(BF16), go)
                g_chances = mm_nt(go, values)
                inner = jnp.sum(chances * g_chances, axis=-1, keepdims=True)
                g_scores = jnp.where(allowed, chances * (g_chances - inner), 0.0).astype(BF16)
                g_queries = join_halves(mm(g_scores, keys)) * HEAD_DIM ** (-0.5)
                g_keys = mm_tn(g_scores, queries) * HEAD_DIM ** (-0.5)
                for part, value in enumerate((g_queries, g_keys, g_values)):
                    low = part * feature + start
                    gt_v[layer, :, low : low + PAIR] = value.astype(BF16)
            put(layer, 3, "gt", gt_v).start()
            small_v[layer, 2:3, :] = column_sum(gt_v[layer, :, :feature])
            small_v[layer, 3:4, :] = column_sum(gt_v[layer, :, 2 * feature :])
            ga = jnp.zeros((length, feature), F32)
            for index in range(joint_count):
                span = slice(index * feature, (index + 1) * feature)
                ga = ga + mm_nt(gt_v[layer, :, span], wj[index][layer])
            saved_copy(layer, 3).wait()
            normed, scale = norm_parts(h_v[layer])
            small_v[layer, 0:1, :] = column_sum(ga * normed)
            small_v[layer, 1:2, :] = column_sum(ga)
            grad_v[...] = grad_v[...] + norm_back(normed, scale, vecs[layer, 0:1, :], ga)
            put(layer, 4, "small", small_v).start()

        layer_loop(one_layer)
        sent[...] = grad_v[...]

        @pl.when(section == 0)
        def _():
            final = pltpu.make_async_copy(grad_v, stash["r"].at[slot], in_sem.at[1])
            final.start()
            final.wait()

        for layer in range(LAYERS):
            for index, (name, value_ref) in enumerate(
                (
                    ("gw", gw_v),
                    ("gu", gu_v),
                    ("gz", gz_v),
                    ("gt", gt_v),
                    ("small", small_v),
                )
            ):
                put(layer, index, name, value_ref).wait()


def backward_step(branch_scale, tick, seeds, arrived, allowed, weights, vecs, saved, stash):
    length, feature = arrived.shape
    joint_count, hidden_count = counts_of(weights, feature)
    hidden = hidden_count * feature
    weights = tuple(pltpu.with_memory_space_constraint(w, pltpu.VMEM) for w in weights)
    scratch = [
        pltpu.VMEM((LAYERS, length, feature), F32),
        pltpu.VMEM((LAYERS, length, feature), F32),
        pltpu.VMEM((LAYERS, length, 3 * feature), BF16),
        pltpu.VMEM((LAYERS, length, hidden), BF16),
        pltpu.VMEM((length, feature), F32),
        pltpu.VMEM((LAYERS, length, feature), BF16),
        pltpu.VMEM((LAYERS, length, hidden), BF16),
        pltpu.VMEM((LAYERS, length, feature), BF16),
        pltpu.VMEM((length, feature), BF16),
        pltpu.VMEM((LAYERS, length, 3 * feature), BF16),
        pltpu.VMEM((LAYERS, 16, feature), F32),
        pltpu.SemaphoreType.DMA((2,)),
        pltpu.SemaphoreType.DMA((LAYERS, 4)),
        pltpu.SemaphoreType.DMA((LAYERS, 5)),
    ]
    leading = 5 + len(weights) + len(saved)
    outs = pl.pallas_call(
        partial(backward_kernel, branch_scale, joint_count, hidden_count),
        out_shape=tuple(pltpu.HBM(s.shape, s.dtype) for s in stash)
        + (pltpu.VMEM((length, feature), F32), jax.ShapeDtypeStruct((1,), jnp.int32)),
        in_specs=[SMEM, ANY, ANY]
        + [VMEM] * (2 + len(weights))
        + [HBM] * (len(saved) + len(stash)),
        out_specs=tuple([HBM] * len(stash) + [VMEM, SMEM]),
        scratch_shapes=scratch,
        input_output_aliases={leading + i: i for i in range(len(stash))},
        compiler_params=pltpu.CompilerParams(vmem_limit_bytes=SCOPED),
        cost_estimate=cost_of(length, weights),
        name="backward_step",
    )(tick, in_hbm(seeds), arrived, allowed, *weights, vecs, *map(in_hbm, saved), *stash)
    return outs[:-2], outs[-2], outs[-1]


def empty_arrays(shapes):
    return pl.pallas_call(
        lambda *refs: None,
        out_shape=tuple(pltpu.HBM(s.shape, s.dtype) for s in shapes),
        out_specs=tuple([HBM] * len(shapes)),
        name="empty_arrays",
    )()


def body(
    tokens,
    cotangent,
    document_lengths,
    valid_counts,
    first_gain,
    first_shift,
    joint_weight,
    query_value_offsets,
    output_weight,
    output_bias,
    second_gain,
    second_shift,
    expand_weight,
    expand_bias,
    contract_weight,
    contract_bias,
):
    sections = lax.axis_size("section")
    replicas = lax.axis_size("dp")
    section = lax.axis_index("section")
    replica = lax.axis_index("dp")
    near = 2 if replicas % 2 == 0 else 1
    far = replicas // near
    group, member = replica // near, replica % near
    micro_count, row_count, length, feature = tokens.shape
    hidden = expand_weight.shape[-1]
    own = micro_count * row_count
    rows = own * far
    branch_scale = (LAYERS * sections) ** (-0.5)
    first, last = section == 0, section == sections - 1
    positions = jnp.arange(length, dtype=jnp.int32)

    lengths = document_lengths.reshape(own, -1)
    live = (positions[None] < valid_counts.reshape(own, 1)).astype(F32)
    edge_own = jnp.where(
        first,
        tokens.reshape(own, length, feature).astype(F32),
        cotangent.reshape(own, length, feature).astype(F32) * live[:, :, None],
    )
    edges, all_lengths = [edge_own], [lengths]
    for shift in range(1, far):
        pairs = [
            (((g + shift) % far) * near + m, g * near + m) for g in range(far) for m in range(near)
        ]
        ends = sorted({0, sections - 1})
        all_lengths.append(lax.ppermute(lengths, "dp", pairs))
        edges.append(
            lax.ppermute(
                edge_own,
                ("section", "dp"),
                [(e * replicas + a, e * replicas + b) for e in ends for a, b in pairs],
            )
        )
    document_ends = jnp.cumsum(jnp.concatenate(all_lengths, axis=0), axis=-1)
    segment = jnp.sum(
        (positions[None, :, None] >= document_ends[:, None, :]).astype(jnp.int32), axis=-1
    )
    causal = positions[:, None] >= positions[None, :]
    allowed = ((segment[:, :, None] == segment[:, None, :]) & causal[None]).astype(F32)

    wide = [
        v.astype(F32)
        for v in (first_gain, first_shift, output_bias, second_gain, second_shift, contract_bias)
    ]
    blank = jnp.zeros_like(wide[0])
    vecs = jnp.stack(wide + [blank, blank], axis=1)
    offsets = query_value_offsets.astype(F32)
    bj = jnp.concatenate([offsets[:, :feature], blank, offsets[:, feature:]], axis=1)[:, None]
    be = expand_bias.astype(F32)[:, None]
    weights = (joint_weight, output_weight, expand_weight, contract_weight)

    def saved(width, dtype):
        return jax.ShapeDtypeStruct((LAYERS, rows, length, width), dtype)

    edge_shape = jax.ShapeDtypeStruct((rows, length, feature), F32)
    row_shape = jax.ShapeDtypeStruct((length, feature), F32)
    forward_shapes = (
        saved(feature, F32),
        saved(feature, F32),
        saved(feature, BF16),
        saved(3 * feature, BF16),
        saved(feature, BF16),
        saved(feature, BF16),
        saved(hidden, BF16),
        saved(hidden, BF16),
        edge_shape,
    )
    backward_shapes = (
        saved(feature, BF16),
        saved(hidden, BF16),
        saved(feature, BF16),
        saved(3 * feature, BF16),
        jax.ShapeDtypeStruct((LAYERS, rows, 16, feature), F32),
        edge_shape,
    )
    made = empty_arrays(forward_shapes + backward_shapes + (row_shape, row_shape))
    forward_stash = made[: len(forward_shapes)]
    backward_stash = made[len(forward_shapes) : -2]
    ticks = rows + 2 * (sections - 1)
    onward = [(i, i + 1) for i in range(sections - 1)]
    back = [(i + 1, i) for i in range(sections - 1)]

    steps = []
    while not steps or steps[-1] > 1:
        steps.append(steps[-1] // 2 if steps else sections // 2)
    mirrored = sections - 1 - section
    even = section % 2 == 0
    arrives = [jnp.where(even, section, mirrored) % (2 * step) == step for step in steps]
    vectors, allowed, even, arrives, first, where, weights = lax.optimization_barrier(
        ((vecs, bj, be), allowed, even, arrives, first, (section, group, member), weights)
    )
    loaded = load_weights(weights)
    chunk = min(ticks, UNROLL)
    rounds = -(-ticks // chunk)
    edge = jnp.concatenate(edges, axis=0) if rounds > 1 else None

    def halve(block, step):
        low, high = jnp.split(block, 2, axis=-1)
        pairs = [(a, a + step) for a in range(0, sections, 2 * step)]
        pairs += [(sections - 1 - a, sections - 1 - b) for a, b in pairs]
        got = lax.ppermute(jnp.where(even, high, low), "section", pairs)
        return jnp.where(even, low, high), got

    def spread(block, level):
        kept, got = halve(block, steps[level])
        if steps[level] == 1:
            return kept, got
        return jnp.where(arrives[level], got, kept)

    def run(step, pairs, stash):
        def turn(carry, source_of):
            stash, sent, arrived, tick = carry
            for index in range(chunk):
                arriving = lax.ppermute(sent, "section", pairs)
                stash, sent, tick = step(tick, source_of(index), arrived, stash)
                arrived = arriving
            return stash, sent, arrived, tick

        start = (stash, made[-2], made[-1], jnp.zeros((1,), jnp.int32))
        if rounds == 1:
            return turn(start, lambda index: edges[min(index, rows - 1) // own])[::3]

        def again(_, carry):
            return turn(carry, lambda index: edge)

        return lax.fori_loop(0, rounds, again, start)[::3]

    forward_stash, walked = run(
        lambda tick, source, arrived, stash: forward_step(
            branch_scale, tick, source, arrived, allowed, loaded, vectors, stash
        ),
        onward,
        forward_stash,
    )
    sh, sg, sa, st, so, sc, sm, sd, final_rows = forward_stash
    backward_stash, walked = run(
        lambda tick, source, arrived, stash: backward_step(
            branch_scale, tick, source, arrived, allowed, loaded, vectors[0], (sh, sg, st, sd), stash
        ),
        back,
        backward_stash,
    )
    backward_stash, (section, group, member), _ = lax.optimization_barrier(
        (backward_stash, where, walked)
    )
    gw, gu, gz, gt, small, first_rows = backward_stash

    def exchange(sends):
        got = []
        for shift, payload in enumerate(sends, 1):
            pairs = [
                (g * near + m, g * near + (m + shift) % near)
                for g in range(far)
                for m in range(near)
            ]
            got.append(lax.ppermute(payload, "dp", pairs))
        return got

    def near_sum(part):
        sends = [part((member + shift) % near) for shift in range(1, near)]
        return sends, lambda got: sum(got, part(member))

    def weight_gradient(left, right):
        width = left.shape[-1]
        share = width // replicas
        left = left.reshape(LAYERS, rows * length, width)
        right = right.reshape(LAYERS, rows * length, right.shape[-1])

        def part(index):
            mine = lax.dynamic_slice_in_dim(left, (group * near + index) * share, share, axis=2)
            return jnp.einsum("lrd,lre->lde", mine, right, preferred_element_type=F32)

        return near_sum(part)

    block = jnp.where(first, first_rows[:own], final_rows[:own])
    pending = []
    for level, (left, right) in enumerate(((sm, gw), (sc, gu), (sa, gt), (so, gz))):
        if level < len(steps):
            block = spread(block, level)
        sends, finish = weight_gradient(left, right)
        if level < len(steps):
            block, sends = lax.optimization_barrier((block, sends))
        pending.append((sends, finish))
    for level in range(len(pending), len(steps)):
        block = spread(block, level)
    kept, got = block
    pending = [finish(exchange(sends)) for sends, finish in pending]
    contract_gradient, expand_gradient, joint_gradient, output_gradient = pending

    sums = jnp.sum(small, axis=1)
    vectors = [
        sums[:, 0],
        sums[:, 1],
        sums[:, 2:4].reshape(LAYERS, 2 * feature),
        sums[:, 6],
        sums[:, 4],
        sums[:, 5],
        sums[:, 8 : 8 + hidden // feature].reshape(LAYERS, hidden),
        sums[:, 7],
    ]
    packed = jnp.concatenate([v.reshape(LAYERS, replicas, -1) for v in vectors], axis=2)
    sends, finish = near_sum(
        lambda index: lax.dynamic_index_in_dim(
            packed, group * near + index, axis=1, keepdims=False
        )
    )
    shared = finish(exchange(sends))
    pieces, at = [], 0
    for v in vectors:
        share = v.shape[1] // replicas
        pieces.append(shared[:, at : at + share])
        at += share

    share = feature // sections
    out_shape = (micro_count, row_count, length, share)
    input_gradient = jnp.where(even, kept, got)
    final_hidden = jnp.where(even, got, kept)
    return (
        final_hidden.reshape(out_shape),
        input_gradient.reshape(out_shape),
        pieces[0],
        pieces[1],
        joint_gradient,
        pieces[2],
        output_gradient,
        pieces[3],
        pieces[4],
        pieces[5],
        expand_gradient,
        pieces[6],
        contract_gradient,
        pieces[7],
    )


def solution(mesh):
    return jax.shard_map(
        body,
        mesh=mesh,
        in_specs=(
            P(None, "dp", None, None),
            P(None, "dp", None, None),
            P(None, "dp", None),
            P(None, "dp"),
            P("section", None),
            P("section", None),
            P("section", None, None),
            P("section", None),
            P("section", None, None),
            P("section", None),
            P("section", None),
            P("section", None),
            P("section", None, None),
            P("section", None),
            P("section", None, None),
            P("section", None),
        ),
        out_specs=(
            P(None, "dp", None, "section"),
            P(None, "dp", None, "section"),
            P("section", "dp"),
            P("section", "dp"),
            P("section", "dp", None),
            P("section", "dp"),
            P("section", "dp", None),
            P("section", "dp"),
            P("section", "dp"),
            P("section", "dp"),
            P("section", "dp", None),
            P("section", "dp"),
            P("section", "dp", None),
            P("section", "dp"),
        ),
        check_vma=False,
    )
```

```python
from functools import partial

import jax
import jax.numpy as jnp
from jax import lax
from jax.experimental import pallas as pl
from jax.experimental.pallas import tpu as pltpu
from jax.sharding import PartitionSpec as P

HEAD_DIM = 64
LAYERS = 2
PAIR = 2 * HEAD_DIM
SCOPED = 10368 * 1024
EPS = 1e-05
BF16 = jnp.bfloat16
F32 = jnp.float32
ANY = pl.BlockSpec(memory_space=pl.ANY)
VMEM = pl.BlockSpec(memory_space=pltpu.VMEM)
HBM = pl.BlockSpec(memory_space=pltpu.HBM)
UNROLL = 22
SMEM = pl.BlockSpec(memory_space=pltpu.SMEM)
TANH_SCALE = 0.7978845608028654


def mm(left, right):
    return lax.dot_general(left, right, (((1,), (0,)), ((), ())), preferred_element_type=F32)


def mm_nt(left, right):
    return lax.dot_general(left, right, (((1,), (1,)), ((), ())), preferred_element_type=F32)


def mm_tn(left, right):
    return lax.dot_general(left, right, (((0,), (0,)), ((), ())), preferred_element_type=F32)


def norm_parts(values):
    center = jnp.mean(values, axis=-1, keepdims=True)
    centered = values - center
    scale = lax.rsqrt(jnp.mean(centered * centered, axis=-1, keepdims=True) + EPS)
    return centered * scale, scale


def norm_back(normed, scale, gain, gradient):
    weighted = gradient * gain
    mean_weighted = jnp.mean(weighted, axis=-1, keepdims=True)
    mean_product = jnp.mean(weighted * normed, axis=-1, keepdims=True)
    return scale * (weighted - mean_weighted - normed * mean_product)


def stack_halves(block):
    low_lanes = lax.broadcasted_iota(jnp.int32, block.shape, 1) < HEAD_DIM
    zero = jnp.zeros_like(block)
    return jnp.concatenate(
        [jnp.where(low_lanes, block, zero), jnp.where(low_lanes, zero, block)], axis=0
    )


def join_halves(stacked):
    length = stacked.shape[0] // 2
    low_lanes = lax.broadcasted_iota(jnp.int32, (length, PAIR), 1) < HEAD_DIM
    return jnp.where(low_lanes, stacked[:length], stacked[length:])


def pair_probabilities(queries, keys, allowed):
    scores = mm_nt(queries, keys) * HEAD_DIM ** (-0.5)
    scores = jnp.where(allowed, scores, -1e30)
    powers = jnp.exp(scores - jnp.max(scores, axis=-1, keepdims=True))
    return powers / jnp.sum(powers, axis=-1, keepdims=True)


def column_sum(values):
    return jnp.sum(values.astype(F32), axis=0, keepdims=True)


def weight_blocks(weights):
    width = weights[1].shape[-1]
    return [
        (index, row, column)
        for index, weight in enumerate(weights)
        for row in range(0, weight.shape[1], width)
        for column in range(0, weight.shape[2], width)
    ]


def load_kernel(blocks, width, *refs):
    weights, targets, sems = refs[:4], refs[4:-1], refs[-1]
    copies = [
        pltpu.make_async_copy(
            weights[index].at[:, row : row + width, column : column + width],
            target,
            sems.at[at],
        )
        for at, ((index, row, column), target) in enumerate(zip(blocks, targets))
    ]
    for copy in copies:
        copy.start()
    for copy in copies:
        copy.wait()


def load_weights(weights):
    width = weights[1].shape[-1]
    blocks = weight_blocks(weights)
    return pl.pallas_call(
        partial(load_kernel, blocks, width),
        out_shape=tuple(pltpu.VMEM((LAYERS, width, width), BF16) for _ in blocks),
        in_specs=[ANY] * 4,
        out_specs=tuple([VMEM] * len(blocks)),
        scratch_shapes=[pltpu.SemaphoreType.DMA((len(blocks),))],
        compiler_params=pltpu.CompilerParams(vmem_limit_bytes=SCOPED),
        name="load_weights",
    )(*map(in_hbm, weights))


def load_turned_kernel(source, *refs):
    targets, sems = refs[:-1], refs[-1]
    copies = [
        pltpu.make_async_copy(source.at[at], target, sems.at[at])
        for at, target in enumerate(targets)
    ]
    for copy in copies:
        copy.start()
    for copy in copies:
        copy.wait()


def load_turned(turned):
    count, _, width, _ = turned.shape
    return pl.pallas_call(
        load_turned_kernel,
        out_shape=tuple(pltpu.VMEM((LAYERS, width, width), BF16) for _ in range(count)),
        in_specs=[ANY],
        out_specs=tuple([VMEM] * count),
        scratch_shapes=[pltpu.SemaphoreType.DMA((count,))],
        compiler_params=pltpu.CompilerParams(vmem_limit_bytes=SCOPED),
        name="load_turned",
    )(in_hbm(turned))


def turn_kernel(blocks, width, late, *refs):
    weights, turned, before_v, after_v, in_sem, out_sem = refs[:4], *refs[5:]
    section = lax.axis_index("section")
    half = lax.axis_size("section") // 2
    chosen = section < half if late else section >= half

    @pl.when(chosen)
    def _():
        turns = [(at, layer) for at in range(len(blocks)) for layer in range(LAYERS)]

        def fetch(step):
            at, layer = turns[step]
            index, row, column = blocks[at]
            return pltpu.make_async_copy(
                weights[index].at[layer, row : row + width, column : column + width],
                before_v.at[step % 2],
                in_sem.at[step % 2],
            )

        def keep(step):
            at, layer = turns[step]
            return pltpu.make_async_copy(
                after_v.at[step % 2], turned.at[at, layer], out_sem.at[step % 2]
            )

        fetch(0).start()
        for step in range(len(turns)):
            fetch(step).wait()
            if step + 1 < len(turns):
                fetch(step + 1).start()
            if step > 1:
                keep(step - 2).wait()
            after_v[step % 2] = before_v[step % 2].T
            keep(step).start()
        keep(len(turns) - 2).wait()
        keep(len(turns) - 1).wait()


def turn_weights(weights, turned, late):
    width = weights[1].shape[-1]
    return pl.pallas_call(
        partial(turn_kernel, weight_blocks(weights), width, late),
        out_shape=pltpu.HBM(turned.shape, BF16),
        in_specs=[ANY] * 4 + [HBM],
        out_specs=HBM,
        scratch_shapes=[
            pltpu.VMEM((2, width, width), BF16),
            pltpu.VMEM((2, width, width), BF16),
            pltpu.SemaphoreType.DMA((2,)),
            pltpu.SemaphoreType.DMA((2,)),
        ],
        input_output_aliases={4: 0},
        compiler_params=pltpu.CompilerParams(vmem_limit_bytes=SCOPED),
        name="turn_weights",
    )(*map(in_hbm, weights), in_hbm(turned))


def in_hbm(value):
    return pltpu.with_memory_space_constraint(value, pltpu.HBM)


def layer_loop(body):
    lax.fori_loop(0, LAYERS, lambda index, carry: (body(index), carry)[1], 0)


def forward_kernel(branch_scale, joint_count, hidden_count, tick, tokens, arrived, allowed_rows, *refs):
    weight_count = joint_count + 1 + 2 * hidden_count
    wj = refs[:joint_count]
    wo = refs[joint_count]
    we = refs[joint_count + 1 : joint_count + 1 + hidden_count]
    wc = refs[joint_count + 1 + hidden_count : weight_count]
    vecs, bj, be = refs[weight_count : weight_count + 3]
    refs = refs[weight_count + 3 :]
    names = ("h", "g", "a", "t", "o", "c", "m", "d", "f")
    stash = dict(zip(names, refs[9:18]))
    sent, next_tick = refs[18:20]
    h_v, g_v, a_v, t_v, o_v, c_v, m_v, d_v, in_sem, out_sem = refs[20:]
    next_tick[0] = tick[0] + 1
    section = lax.axis_index("section")
    last = section == lax.axis_size("section") - 1
    feature = tokens.shape[-1]
    rows = allowed_rows.shape[0]
    row_index = tick[0] - 2 * section

    @pl.when((row_index >= 0) & (row_index < rows))
    def _():
        slot = jnp.clip(row_index, 0, rows - 1)

        @pl.when(section == 0)
        def _():
            pltpu.make_async_copy(tokens.at[lax.rem(slot, tokens.shape[0])], h_v.at[0], in_sem.at[0]).start()

        @pl.when(section > 0)
        def _():
            pltpu.make_async_copy(arrived, h_v.at[0], in_sem.at[0]).start()

        def put(layer, index, name, value_ref):
            return pltpu.make_async_copy(
                value_ref.at[layer], stash[name].at[layer, slot], out_sem.at[layer, index]
            )

        allowed = jnp.concatenate([allowed_rows[slot], allowed_rows[slot]], axis=0) > 0.5
        pltpu.make_async_copy(arrived, h_v.at[0], in_sem.at[0]).wait()

        def one_layer(layer):
            put(layer, 0, "h", h_v).start()
            row = h_v[layer]
            normed, _ = norm_parts(row)
            a_low = (normed * vecs[layer, 0:1, :] + vecs[layer, 1:2, :]).astype(BF16)
            a_v[layer] = a_low
            put(layer, 2, "a", a_v).start()
            for index in range(joint_count):
                span = slice(index * feature, (index + 1) * feature)
                t_v[layer, :, span] = (
                    mm(a_low, wj[index][layer]) + bj[layer, :, span]
                ).astype(BF16)
            put(layer, 3, "t", t_v).start()
            for start in range(0, feature, PAIR):
                queries = stack_halves(t_v[layer, :, start : start + PAIR])
                keys = t_v[layer, :, feature + start : feature + start + PAIR]
                values = t_v[layer, :, 2 * feature + start : 2 * feature + start + PAIR]
                chances = pair_probabilities(queries, keys, allowed).astype(BF16)
                o_v[layer, :, start : start + PAIR] = join_halves(mm(chances, values)).astype(BF16)
            put(layer, 4, "o", o_v).start()
            mixed = row + branch_scale * (mm(o_v[layer], wo[layer]) + vecs[layer, 2:3, :])
            g_v[layer] = mixed
            put(layer, 1, "g", g_v).start()
            normed, _ = norm_parts(mixed)
            c_low = (normed * vecs[layer, 3:4, :] + vecs[layer, 4:5, :]).astype(BF16)
            c_v[layer] = c_low
            put(layer, 5, "c", c_v).start()
            for index in range(hidden_count):
                span = slice(index * feature, (index + 1) * feature)
                u = mm(c_low, we[index][layer]) + be[layer, :, span]
                square = u * u
                th = jnp.tanh(TANH_SCALE * (u + 0.044715 * (square * u)))
                half = 0.5 * (1.0 + th)
                m_v[layer, :, span] = (u * half).astype(BF16)
                slope = half + 0.5 * u * (1.0 - th * th) * (
                    TANH_SCALE * (1.0 + 3.0 * 0.044715 * square)
                )
                d_v[layer, :, span] = slope.astype(BF16)
            put(layer, 6, "m", m_v).start()
            put(layer, 7, "d", d_v).start()
            z = vecs[layer, 5:6, :]
            for index in range(hidden_count):
                span = slice(index * feature, (index + 1) * feature)
                z = z + mm(m_v[layer, :, span], wc[index][layer])
            h_v[layer + 1] = mixed + branch_scale * z

        layer_loop(one_layer)
        sent[...] = h_v[LAYERS]

        @pl.when(last)
        def _():
            final = pltpu.make_async_copy(h_v.at[LAYERS], stash["f"].at[slot], in_sem.at[1])
            final.start()
            final.wait()

        for layer in range(LAYERS):
            for index, (name, value_ref) in enumerate(
                (
                    ("h", h_v),
                    ("g", g_v),
                    ("a", a_v),
                    ("t", t_v),
                    ("o", o_v),
                    ("c", c_v),
                    ("m", m_v),
                    ("d", d_v),
                )
            ):
                put(layer, index, name, value_ref).wait()


def counts_of(weights, feature):
    hidden_count = (len(weights) - 4) // 2
    return 3, hidden_count


def cost_of(length, weights):
    return pl.CostEstimate(
        flops=2 * length * sum(w.size for w in weights),
        bytes_accessed=2 * sum(w.size for w in weights),
        transcendentals=0,
    )


def forward_step(branch_scale, tick, tokens, arrived, allowed, weights, vectors, stash):
    length, feature = arrived.shape
    joint_count, hidden_count = counts_of(weights, feature)
    hidden = hidden_count * feature
    weights = tuple(pltpu.with_memory_space_constraint(w, pltpu.VMEM) for w in weights)
    scratch = [
        pltpu.VMEM((LAYERS + 1, length, feature), F32),
        pltpu.VMEM((LAYERS, length, feature), F32),
        pltpu.VMEM((LAYERS, length, feature), BF16),
        pltpu.VMEM((LAYERS, length, 3 * feature), BF16),
        pltpu.VMEM((LAYERS, length, feature), BF16),
        pltpu.VMEM((LAYERS, length, feature), BF16),
        pltpu.VMEM((LAYERS, length, hidden), BF16),
        pltpu.VMEM((LAYERS, length, hidden), BF16),
        pltpu.SemaphoreType.DMA((2,)),
        pltpu.SemaphoreType.DMA((LAYERS, 8)),
    ]
    leading = 4 + len(weights) + len(vectors)
    outs = pl.pallas_call(
        partial(forward_kernel, branch_scale, joint_count, hidden_count),
        out_shape=tuple(pltpu.HBM(s.shape, s.dtype) for s in stash)
        + (pltpu.VMEM((length, feature), F32), jax.ShapeDtypeStruct((1,), jnp.int32)),
        in_specs=[SMEM, ANY, ANY]
        + [VMEM] * (1 + len(weights) + len(vectors))
        + [HBM] * len(stash),
        out_specs=tuple([HBM] * len(stash) + [VMEM, SMEM]),
        scratch_shapes=scratch,
        input_output_aliases={leading + i: i for i in range(len(stash))},
        compiler_params=pltpu.CompilerParams(vmem_limit_bytes=SCOPED),
        cost_estimate=cost_of(length, weights),
        name="forward_step",
    )(tick, in_hbm(tokens), arrived, allowed, *weights, *vectors, *stash)
    return outs[:-2], outs[-2], outs[-1]


def backward_kernel(branch_scale, joint_count, hidden_count, tick, seeds, arrived, allowed_rows, *refs):
    weight_count = joint_count + 1 + 2 * hidden_count
    wj = refs[:joint_count]
    wo = refs[joint_count]
    we = refs[joint_count + 1 : joint_count + 1 + hidden_count]
    wc = refs[joint_count + 1 + hidden_count : weight_count]
    vecs, sh, sg, st, sd = refs[weight_count : weight_count + 5]
    refs = refs[weight_count + 5 :]
    names = ("gw", "gu", "gz", "gt", "small", "r")
    stash = dict(zip(names, refs[6:12]))
    sent, next_tick = refs[12:14]
    (
        h_v,
        g_v,
        t_v,
        d_v,
        grad_v,
        gw_v,
        gu_v,
        gz_v,
        go_v,
        gt_v,
        small_v,
        in_sem,
        s_sem,
        out_sem,
    ) = refs[14:]
    next_tick[0] = tick[0] + 1
    section = lax.axis_index("section")
    sections = lax.axis_size("section")
    _, length, feature = seeds.shape
    rows = allowed_rows.shape[0]
    row_index = tick[0] - 2 * (sections - 1 - section)

    @pl.when((row_index >= 0) & (row_index < rows))
    def _():
        slot = jnp.clip(row_index, 0, rows - 1)

        @pl.when(section == sections - 1)
        def _():
            pltpu.make_async_copy(seeds.at[lax.rem(slot, seeds.shape[0])], grad_v, in_sem.at[0]).start()

        @pl.when(section < sections - 1)
        def _():
            pltpu.make_async_copy(arrived, grad_v, in_sem.at[0]).start()

        saved = ((sd, d_v), (sg, g_v), (st, t_v), (sh, h_v))

        def saved_copy(layer, index):
            source, target = saved[index]
            return pltpu.make_async_copy(
                source.at[layer, slot], target.at[layer], s_sem.at[layer, index]
            )

        for layer in reversed(range(LAYERS)):
            for index in range(4):
                saved_copy(layer, index).start()

        def put(layer, index, name, value_ref):
            return pltpu.make_async_copy(
                value_ref.at[layer], stash[name].at[layer, slot], out_sem.at[layer, index]
            )

        allowed = jnp.concatenate([allowed_rows[slot], allowed_rows[slot]], axis=0) > 0.5
        pltpu.make_async_copy(arrived, grad_v, in_sem.at[0]).wait()

        def one_layer(turn):
            layer = LAYERS - 1 - turn
            gw = (branch_scale * grad_v[...]).astype(BF16)
            gw_v[layer] = gw
            put(layer, 0, "gw", gw_v).start()
            small_v[layer, 7:8, :] = column_sum(gw)
            saved_copy(layer, 0).wait()
            gc = jnp.zeros((length, feature), F32)
            for index in range(hidden_count):
                span = slice(index * feature, (index + 1) * feature)
                gu = (d_v[layer, :, span].astype(F32) * mm(gw, wc[index][layer])).astype(BF16)
                gu_v[layer, :, span] = gu
                small_v[layer, 8 + index : 9 + index, :] = column_sum(gu)
            put(layer, 1, "gu", gu_v).start()
            for index in range(hidden_count):
                span = slice(index * feature, (index + 1) * feature)
                gc = gc + mm(gu_v[layer, :, span], we[index][layer])
            saved_copy(layer, 1).wait()
            normed, scale = norm_parts(g_v[layer])
            small_v[layer, 4:5, :] = column_sum(gc * normed)
            small_v[layer, 5:6, :] = column_sum(gc)
            gg = grad_v[...] + norm_back(normed, scale, vecs[layer, 3:4, :], gc)
            grad_v[...] = gg
            gz = (branch_scale * gg).astype(BF16)
            gz_v[layer] = gz
            put(layer, 2, "gz", gz_v).start()
            small_v[layer, 6:7, :] = column_sum(gz)
            go_v[...] = mm(gz, wo[layer]).astype(BF16)
            saved_copy(layer, 2).wait()
            for start in range(0, feature, PAIR):
                queries = stack_halves(t_v[layer, :, start : start + PAIR])
                keys = t_v[layer, :, feature + start : feature + start + PAIR]
                values = t_v[layer, :, 2 * feature + start : 2 * feature + start + PAIR]
                go = stack_halves(go_v[:, start : start + PAIR])
                chances = pair_probabilities(queries, keys, allowed)
                g_values = mm_tn(chances.astype(BF16), go)
                g_chances = mm_nt(go, values)
                inner = jnp.sum(chances * g_chances, axis=-1, keepdims=True)
                g_scores = jnp.where(allowed, chances * (g_chances - inner), 0.0).astype(BF16)
                g_queries = join_halves(mm(g_scores, keys)) * HEAD_DIM ** (-0.5)
                g_keys = mm_tn(g_scores, queries) * HEAD_DIM ** (-0.5)
                for part, value in enumerate((g_queries, g_keys, g_values)):
                    low = part * feature + start
                    gt_v[layer, :, low : low + PAIR] = value.astype(BF16)
            put(layer, 3, "gt", gt_v).start()
            small_v[layer, 2:3, :] = column_sum(gt_v[layer, :, :feature])
            small_v[layer, 3:4, :] = column_sum(gt_v[layer, :, 2 * feature :])
            ga = jnp.zeros((length, feature), F32)
            for index in range(joint_count):
                span = slice(index * feature, (index + 1) * feature)
                ga = ga + mm(gt_v[layer, :, span], wj[index][layer])
            saved_copy(layer, 3).wait()
            normed, scale = norm_parts(h_v[layer])
            small_v[layer, 0:1, :] = column_sum(ga * normed)
            small_v[layer, 1:2, :] = column_sum(ga)
            grad_v[...] = grad_v[...] + norm_back(normed, scale, vecs[layer, 0:1, :], ga)
            put(layer, 4, "small", small_v).start()

        layer_loop(one_layer)
        sent[...] = grad_v[...]

        @pl.when(section == 0)
        def _():
            final = pltpu.make_async_copy(grad_v, stash["r"].at[slot], in_sem.at[1])
            final.start()
            final.wait()

        for layer in range(LAYERS):
            for index, (name, value_ref) in enumerate(
                (
                    ("gw", gw_v),
                    ("gu", gu_v),
                    ("gz", gz_v),
                    ("gt", gt_v),
                    ("small", small_v),
                )
            ):
                put(layer, index, name, value_ref).wait()


def backward_step(branch_scale, tick, seeds, arrived, allowed, weights, vecs, saved, stash):
    length, feature = arrived.shape
    joint_count, hidden_count = counts_of(weights, feature)
    hidden = hidden_count * feature
    weights = tuple(pltpu.with_memory_space_constraint(w, pltpu.VMEM) for w in weights)
    scratch = [
        pltpu.VMEM((LAYERS, length, feature), F32),
        pltpu.VMEM((LAYERS, length, feature), F32),
        pltpu.VMEM((LAYERS, length, 3 * feature), BF16),
        pltpu.VMEM((LAYERS, length, hidden), BF16),
        pltpu.VMEM((length, feature), F32),
        pltpu.VMEM((LAYERS, length, feature), BF16),
        pltpu.VMEM((LAYERS, length, hidden), BF16),
        pltpu.VMEM((LAYERS, length, feature), BF16),
        pltpu.VMEM((length, feature), BF16),
        pltpu.VMEM((LAYERS, length, 3 * feature), BF16),
        pltpu.VMEM((LAYERS, 16, feature), F32),
        pltpu.SemaphoreType.DMA((2,)),
        pltpu.SemaphoreType.DMA((LAYERS, 4)),
        pltpu.SemaphoreType.DMA((LAYERS, 5)),
    ]
    leading = 5 + len(weights) + len(saved)
    outs = pl.pallas_call(
        partial(backward_kernel, branch_scale, joint_count, hidden_count),
        out_shape=tuple(pltpu.HBM(s.shape, s.dtype) for s in stash)
        + (pltpu.VMEM((length, feature), F32), jax.ShapeDtypeStruct((1,), jnp.int32)),
        in_specs=[SMEM, ANY, ANY]
        + [VMEM] * (2 + len(weights))
        + [HBM] * (len(saved) + len(stash)),
        out_specs=tuple([HBM] * len(stash) + [VMEM, SMEM]),
        scratch_shapes=scratch,
        input_output_aliases={leading + i: i for i in range(len(stash))},
        compiler_params=pltpu.CompilerParams(vmem_limit_bytes=SCOPED),
        cost_estimate=cost_of(length, weights),
        name="backward_step",
    )(tick, in_hbm(seeds), arrived, allowed, *weights, vecs, *map(in_hbm, saved), *stash)
    return outs[:-2], outs[-2], outs[-1]


def empty_arrays(shapes):
    return pl.pallas_call(
        lambda *refs: None,
        out_shape=tuple(pltpu.HBM(s.shape, s.dtype) for s in shapes),
        out_specs=tuple([HBM] * len(shapes)),
        name="empty_arrays",
    )()


def body(
    tokens,
    cotangent,
    document_lengths,
    valid_counts,
    first_gain,
    first_shift,
    joint_weight,
    query_value_offsets,
    output_weight,
    output_bias,
    second_gain,
    second_shift,
    expand_weight,
    expand_bias,
    contract_weight,
    contract_bias,
):
    sections = lax.axis_size("section")
    replicas = lax.axis_size("dp")
    section = lax.axis_index("section")
    replica = lax.axis_index("dp")
    near = 2 if replicas % 2 == 0 else 1
    far = replicas // near
    group, member = replica // near, replica % near
    micro_count, row_count, length, feature = tokens.shape
    hidden = expand_weight.shape[-1]
    own = micro_count * row_count
    rows = own * far
    branch_scale = (LAYERS * sections) ** (-0.5)
    first, last = section == 0, section == sections - 1
    positions = jnp.arange(length, dtype=jnp.int32)

    lengths = document_lengths.reshape(own, -1)
    live = (positions[None] < valid_counts.reshape(own, 1)).astype(F32)
    edge_own = jnp.where(
        first,
        tokens.reshape(own, length, feature).astype(F32),
        cotangent.reshape(own, length, feature).astype(F32) * live[:, :, None],
    )
    edges, all_lengths = [edge_own], [lengths]
    for shift in range(1, far):
        pairs = [
            (((g + shift) % far) * near + m, g * near + m) for g in range(far) for m in range(near)
        ]
        ends = sorted({0, sections - 1})
        all_lengths.append(lax.ppermute(lengths, "dp", pairs))
        edges.append(
            lax.ppermute(
                edge_own,
                ("section", "dp"),
                [(e * replicas + a, e * replicas + b) for e in ends for a, b in pairs],
            )
        )
    document_ends = jnp.cumsum(jnp.concatenate(all_lengths, axis=0), axis=-1)
    segment = jnp.sum(
        (positions[None, :, None] >= document_ends[:, None, :]).astype(jnp.int32), axis=-1
    )
    causal = positions[:, None] >= positions[None, :]
    allowed = ((segment[:, :, None] == segment[:, None, :]) & causal[None]).astype(F32)

    wide = [
        v.astype(F32)
        for v in (first_gain, first_shift, output_bias, second_gain, second_shift, contract_bias)
    ]
    blank = jnp.zeros_like(wide[0])
    vecs = jnp.stack(wide + [blank, blank], axis=1)
    offsets = query_value_offsets.astype(F32)
    bj = jnp.concatenate([offsets[:, :feature], blank, offsets[:, feature:]], axis=1)[:, None]
    be = expand_bias.astype(F32)[:, None]
    weights = (joint_weight, output_weight, expand_weight, contract_weight)

    def saved(width, dtype):
        return jax.ShapeDtypeStruct((LAYERS, rows, length, width), dtype)

    edge_shape = jax.ShapeDtypeStruct((rows, length, feature), F32)
    row_shape = jax.ShapeDtypeStruct((length, feature), F32)
    forward_shapes = (
        saved(feature, F32),
        saved(feature, F32),
        saved(feature, BF16),
        saved(3 * feature, BF16),
        saved(feature, BF16),
        saved(feature, BF16),
        saved(hidden, BF16),
        saved(hidden, BF16),
        edge_shape,
    )
    backward_shapes = (
        saved(feature, BF16),
        saved(hidden, BF16),
        saved(feature, BF16),
        saved(3 * feature, BF16),
        jax.ShapeDtypeStruct((LAYERS, rows, 16, feature), F32),
        edge_shape,
    )
    width = output_weight.shape[-1]
    turned_shape = jax.ShapeDtypeStruct(
        (len(weight_blocks(weights)), LAYERS, width, width), BF16
    )
    made = empty_arrays(forward_shapes + backward_shapes + (turned_shape, row_shape, row_shape))
    forward_stash = made[: len(forward_shapes)]
    backward_stash = made[len(forward_shapes) : -3]
    ticks = rows + 2 * (sections - 1)
    onward = [(i, i + 1) for i in range(sections - 1)]
    back = [(i + 1, i) for i in range(sections - 1)]

    steps = []
    while not steps or steps[-1] > 1:
        steps.append(steps[-1] // 2 if steps else sections // 2)
    mirrored = sections - 1 - section
    even = section % 2 == 0
    arrives = [jnp.where(even, section, mirrored) % (2 * step) == step for step in steps]
    vectors, allowed, even, arrives, first, where, weights = lax.optimization_barrier(
        ((vecs, bj, be), allowed, even, arrives, first, (section, group, member), weights)
    )
    turned = turn_weights(weights, made[-3], False)
    weights, turned = lax.optimization_barrier((weights, turned))
    loaded = load_weights(weights)
    chunk = min(ticks, UNROLL)
    rounds = -(-ticks // chunk)
    edge = jnp.concatenate(edges, axis=0) if rounds > 1 else None

    def halve(block, step):
        low, high = jnp.split(block, 2, axis=-1)
        pairs = [(a, a + step) for a in range(0, sections, 2 * step)]
        pairs += [(sections - 1 - a, sections - 1 - b) for a, b in pairs]
        got = lax.ppermute(jnp.where(even, high, low), "section", pairs)
        return jnp.where(even, low, high), got

    def spread(block, level):
        kept, got = halve(block, steps[level])
        if steps[level] == 1:
            return kept, got
        return jnp.where(arrives[level], got, kept)

    def run(step, pairs, stash):
        def turn(carry, source_of):
            stash, sent, arrived, tick = carry
            for index in range(chunk):
                arriving = lax.ppermute(sent, "section", pairs)
                stash, sent, tick = step(tick, source_of(index), arrived, stash)
                arrived = arriving
            return stash, sent, arrived, tick

        start = (stash, made[-2], made[-1], jnp.zeros((1,), jnp.int32))
        if rounds == 1:
            return turn(start, lambda index: edges[min(index, rows - 1) // own])[::3]

        def again(_, carry):
            return turn(carry, lambda index: edge)

        return lax.fori_loop(0, rounds, again, start)[::3]

    forward_stash, walked = run(
        lambda tick, source, arrived, stash: forward_step(
            branch_scale, tick, source, arrived, allowed, loaded, vectors, stash
        ),
        onward,
        forward_stash,
    )
    sh, sg, sa, st, so, sc, sm, sd, final_rows = forward_stash
    weights, turned, _ = lax.optimization_barrier((weights, turned, walked))
    loaded = load_turned(turn_weights(weights, turned, True))
    backward_stash, walked = run(
        lambda tick, source, arrived, stash: backward_step(
            branch_scale, tick, source, arrived, allowed, loaded, vectors[0], (sh, sg, st, sd), stash
        ),
        back,
        backward_stash,
    )
    backward_stash, (section, group, member), _ = lax.optimization_barrier(
        (backward_stash, where, walked)
    )
    gw, gu, gz, gt, small, first_rows = backward_stash

    def exchange(sends):
        got = []
        for shift, payload in enumerate(sends, 1):
            pairs = [
                (g * near + m, g * near + (m + shift) % near)
                for g in range(far)
                for m in range(near)
            ]
            got.append(lax.ppermute(payload, "dp", pairs))
        return got

    def near_sum(part):
        sends = [part((member + shift) % near) for shift in range(1, near)]
        return sends, lambda got: sum(got, part(member))

    def weight_gradient(left, right):
        width = left.shape[-1]
        share = width // replicas
        left = left.reshape(LAYERS, rows * length, width)
        right = right.reshape(LAYERS, rows * length, right.shape[-1])

        def part(index):
            mine = lax.dynamic_slice_in_dim(left, (group * near + index) * share, share, axis=2)
            return jnp.einsum("lrd,lre->lde", mine, right, preferred_element_type=F32)

        return near_sum(part)

    block = jnp.where(first, first_rows[:own], final_rows[:own])
    pending = []
    for level, (left, right) in enumerate(((sm, gw), (sc, gu), (sa, gt), (so, gz))):
        if level < len(steps):
            block = spread(block, level)
        sends, finish = weight_gradient(left, right)
        if level < len(steps):
            block, sends = lax.optimization_barrier((block, sends))
        pending.append((sends, finish))
    for level in range(len(pending), len(steps)):
        block = spread(block, level)
    kept, got = block
    pending = [finish(exchange(sends)) for sends, finish in pending]
    contract_gradient, expand_gradient, joint_gradient, output_gradient = pending

    sums = jnp.sum(small, axis=1)
    vectors = [
        sums[:, 0],
        sums[:, 1],
        sums[:, 2:4].reshape(LAYERS, 2 * feature),
        sums[:, 6],
        sums[:, 4],
        sums[:, 5],
        sums[:, 8 : 8 + hidden // feature].reshape(LAYERS, hidden),
        sums[:, 7],
    ]
    packed = jnp.concatenate([v.reshape(LAYERS, replicas, -1) for v in vectors], axis=2)
    sends, finish = near_sum(
        lambda index: lax.dynamic_index_in_dim(
            packed, group * near + index, axis=1, keepdims=False
        )
    )
    shared = finish(exchange(sends))
    pieces, at = [], 0
    for v in vectors:
        share = v.shape[1] // replicas
        pieces.append(shared[:, at : at + share])
        at += share

    share = feature // sections
    out_shape = (micro_count, row_count, length, share)
    input_gradient = jnp.where(even, kept, got)
    final_hidden = jnp.where(even, got, kept)
    return (
        final_hidden.reshape(out_shape),
        input_gradient.reshape(out_shape),
        pieces[0],
        pieces[1],
        joint_gradient,
        pieces[2],
        output_gradient,
        pieces[3],
        pieces[4],
        pieces[5],
        expand_gradient,
        pieces[6],
        contract_gradient,
        pieces[7],
    )


def solution(mesh):
    return jax.shard_map(
        body,
        mesh=mesh,
        in_specs=(
            P(None, "dp", None, None),
            P(None, "dp", None, None),
            P(None, "dp", None),
            P(None, "dp"),
            P("section", None),
            P("section", None),
            P("section", None, None),
            P("section", None),
            P("section", None, None),
            P("section", None),
            P("section", None),
            P("section", None),
            P("section", None, None),
            P("section", None),
            P("section", None, None),
            P("section", None),
        ),
        out_specs=(
            P(None, "dp", None, "section"),
            P(None, "dp", None, "section"),
            P("section", "dp"),
            P("section", "dp"),
            P("section", "dp", None),
            P("section", "dp"),
            P("section", "dp", None),
            P("section", "dp"),
            P("section", "dp"),
            P("section", "dp"),
            P("section", "dp", None),
            P("section", "dp"),
            P("section", "dp", None),
            P("section", "dp"),
        ),
        check_vma=False,
    )
```

```python
from functools import partial

import jax
import jax.numpy as jnp
from jax import lax
from jax.experimental import pallas as pl
from jax.experimental.pallas import tpu as pltpu
from jax.sharding import PartitionSpec as P

HEAD_DIM = 64
LAYERS = 2
PAIR = 2 * HEAD_DIM
SCOPED = 10752 * 1024
EPS = 1e-05
BF16 = jnp.bfloat16
F32 = jnp.float32
ANY = pl.BlockSpec(memory_space=pl.ANY)
VMEM = pl.BlockSpec(memory_space=pltpu.VMEM)
HBM = pl.BlockSpec(memory_space=pltpu.HBM)
UNROLL = 22
SMEM = pl.BlockSpec(memory_space=pltpu.SMEM)
TANH_SCALE = 0.7978845608028654


def mm(left, right):
    return lax.dot_general(left, right, (((1,), (0,)), ((), ())), preferred_element_type=F32)


def mm_nt(left, right):
    return lax.dot_general(left, right, (((1,), (1,)), ((), ())), preferred_element_type=F32)


def mm_tn(left, right):
    return lax.dot_general(left, right, (((0,), (0,)), ((), ())), preferred_element_type=F32)


def norm_parts(values):
    center = jnp.mean(values, axis=-1, keepdims=True)
    centered = values - center
    scale = lax.rsqrt(jnp.mean(centered * centered, axis=-1, keepdims=True) + EPS)
    return centered * scale, scale


def norm_back(normed, scale, gain, gradient):
    weighted = gradient * gain
    mean_weighted = jnp.mean(weighted, axis=-1, keepdims=True)
    mean_product = jnp.mean(weighted * normed, axis=-1, keepdims=True)
    return scale * (weighted - mean_weighted - normed * mean_product)


def stack_halves(block):
    low_lanes = lax.broadcasted_iota(jnp.int32, block.shape, 1) < HEAD_DIM
    zero = jnp.zeros_like(block)
    return jnp.concatenate(
        [jnp.where(low_lanes, block, zero), jnp.where(low_lanes, zero, block)], axis=0
    )


def join_halves(stacked):
    length = stacked.shape[0] // 2
    low_lanes = lax.broadcasted_iota(jnp.int32, (length, PAIR), 1) < HEAD_DIM
    return jnp.where(low_lanes, stacked[:length], stacked[length:])


def pair_probabilities(queries, keys, allowed):
    scores = mm_nt(queries, keys) * HEAD_DIM ** (-0.5)
    scores = jnp.where(allowed, scores, -1e30)
    powers = jnp.exp(scores - jnp.max(scores, axis=-1, keepdims=True))
    return powers / jnp.sum(powers, axis=-1, keepdims=True)


def column_sum(values):
    return jnp.sum(values.astype(F32), axis=0, keepdims=True)


def weight_blocks(weights):
    width = weights[1].shape[-1]
    return [
        (index, row, column)
        for index, weight in enumerate(weights)
        for row in range(0, weight.shape[1], width)
        for column in range(0, weight.shape[2], width)
    ]


def load_kernel(blocks, width, *refs):
    weights, targets, sems = refs[:4], refs[4:-1], refs[-1]
    copies = [
        pltpu.make_async_copy(
            weights[index].at[:, row : row + width, column : column + width],
            target,
            sems.at[at],
        )
        for at, ((index, row, column), target) in enumerate(zip(blocks, targets))
    ]
    for copy in copies:
        copy.start()
    for copy in copies:
        copy.wait()


def load_weights(weights):
    width = weights[1].shape[-1]
    blocks = weight_blocks(weights)
    return pl.pallas_call(
        partial(load_kernel, blocks, width),
        out_shape=tuple(pltpu.VMEM((LAYERS, width, width), BF16) for _ in blocks),
        in_specs=[ANY] * 4,
        out_specs=tuple([VMEM] * len(blocks)),
        scratch_shapes=[pltpu.SemaphoreType.DMA((len(blocks),))],
        compiler_params=pltpu.CompilerParams(vmem_limit_bytes=SCOPED),
        name="load_weights",
    )(*map(in_hbm, weights))


def load_turned_kernel(source, *refs):
    targets, sems = refs[:-1], refs[-1]
    copies = [
        pltpu.make_async_copy(source.at[at], target, sems.at[at])
        for at, target in enumerate(targets)
    ]
    for copy in copies:
        copy.start()
    for copy in copies:
        copy.wait()


def load_turned(turned):
    count, _, width, _ = turned.shape
    return pl.pallas_call(
        load_turned_kernel,
        out_shape=tuple(pltpu.VMEM((LAYERS, width, width), BF16) for _ in range(count)),
        in_specs=[ANY],
        out_specs=tuple([VMEM] * count),
        scratch_shapes=[pltpu.SemaphoreType.DMA((count,))],
        compiler_params=pltpu.CompilerParams(vmem_limit_bytes=SCOPED),
        name="load_turned",
    )(in_hbm(turned))


def turn_kernel(blocks, width, late, *refs):
    weights, turned, before_v, after_v, in_sem, out_sem = refs[:4], *refs[6:]
    section = lax.axis_index("section")
    half = lax.axis_size("section") // 2
    chosen = section < half if late else section >= half

    @pl.when(chosen)
    def _():
        turns = [(at, layer) for at in range(len(blocks)) for layer in range(LAYERS)]

        def fetch(step):
            at, layer = turns[step]
            index, row, column = blocks[at]
            return pltpu.make_async_copy(
                weights[index].at[layer, row : row + width, column : column + width],
                before_v.at[step % 2],
                in_sem.at[step % 2],
            )

        def keep(step):
            at, layer = turns[step]
            return pltpu.make_async_copy(
                after_v.at[step % 2], turned.at[at, layer], out_sem.at[step % 2]
            )

        fetch(0).start()
        for step in range(len(turns)):
            fetch(step).wait()
            if step + 1 < len(turns):
                fetch(step + 1).start()
            if step > 1:
                keep(step - 2).wait()
            after_v[step % 2] = before_v[step % 2].T
            keep(step).start()
        keep(len(turns) - 2).wait()
        keep(len(turns) - 1).wait()


def turn_weights(weights, turned, tick, late):
    width = weights[1].shape[-1]
    return pl.pallas_call(
        partial(turn_kernel, weight_blocks(weights), width, late),
        out_shape=pltpu.HBM(turned.shape, BF16),
        in_specs=[ANY] * 4 + [HBM, ANY],
        out_specs=HBM,
        scratch_shapes=[
            pltpu.VMEM((2, width, width), BF16),
            pltpu.VMEM((2, width, width), BF16),
            pltpu.SemaphoreType.DMA((2,)),
            pltpu.SemaphoreType.DMA((2,)),
        ],
        input_output_aliases={4: 0},
        compiler_params=pltpu.CompilerParams(vmem_limit_bytes=SCOPED),
        name="turn_weights",
    )(*map(in_hbm, weights), in_hbm(turned), tick)


def in_hbm(value):
    return pltpu.with_memory_space_constraint(value, pltpu.HBM)


def layer_loop(body):
    lax.fori_loop(0, LAYERS, lambda index, carry: (body(index), carry)[1], 0)


def forward_kernel(branch_scale, joint_count, hidden_count, tick, tokens, arrived, allowed_rows, *refs):
    weight_count = joint_count + 1 + 2 * hidden_count
    wj = refs[:joint_count]
    wo = refs[joint_count]
    we = refs[joint_count + 1 : joint_count + 1 + hidden_count]
    wc = refs[joint_count + 1 + hidden_count : weight_count]
    vecs, bj, be = refs[weight_count : weight_count + 3]
    refs = refs[weight_count + 3 :]
    names = ("h", "g", "a", "t", "o", "c", "m", "d", "f")
    stash = dict(zip(names, refs[9:18]))
    sent, next_tick = refs[18:20]
    h_v, g_v, a_v, t_v, o_v, c_v, m_v, d_v, in_sem, out_sem = refs[20:]
    next_tick[0] = tick[0] + 1
    section = lax.axis_index("section")
    last = section == lax.axis_size("section") - 1
    feature = tokens.shape[-1]
    rows = allowed_rows.shape[0]
    row_index = tick[0] - 2 * section

    @pl.when((row_index >= 0) & (row_index < rows))
    def _():
        slot = jnp.clip(row_index, 0, rows - 1)

        @pl.when(section == 0)
        def _():
            pltpu.make_async_copy(tokens.at[lax.rem(slot, tokens.shape[0])], h_v.at[0], in_sem.at[0]).start()

        @pl.when(section > 0)
        def _():
            pltpu.make_async_copy(arrived, h_v.at[0], in_sem.at[0]).start()

        def put(layer, index, name, value_ref):
            return pltpu.make_async_copy(
                value_ref.at[layer], stash[name].at[layer, slot], out_sem.at[layer, index]
            )

        allowed = jnp.concatenate([allowed_rows[slot], allowed_rows[slot]], axis=0) > 0.5
        pltpu.make_async_copy(arrived, h_v.at[0], in_sem.at[0]).wait()

        def one_layer(layer):
            put(layer, 0, "h", h_v).start()
            row = h_v[layer]
            normed, _ = norm_parts(row)
            a_low = (normed * vecs[layer, 0:1, :] + vecs[layer, 1:2, :]).astype(BF16)
            a_v[layer] = a_low
            put(layer, 2, "a", a_v).start()
            for index in range(joint_count):
                span = slice(index * feature, (index + 1) * feature)
                t_v[layer, :, span] = (
                    mm(a_low, wj[index][layer]) + bj[layer, :, span]
                ).astype(BF16)
            put(layer, 3, "t", t_v).start()
            for start in range(0, feature, PAIR):
                queries = stack_halves(t_v[layer, :, start : start + PAIR])
                keys = t_v[layer, :, feature + start : feature + start + PAIR]
                values = t_v[layer, :, 2 * feature + start : 2 * feature + start + PAIR]
                chances = pair_probabilities(queries, keys, allowed).astype(BF16)
                o_v[layer, :, start : start + PAIR] = join_halves(mm(chances, values)).astype(BF16)
            put(layer, 4, "o", o_v).start()
            mixed = row + branch_scale * (mm(o_v[layer], wo[layer]) + vecs[layer, 2:3, :])
            g_v[layer] = mixed
            put(layer, 1, "g", g_v).start()
            normed, _ = norm_parts(mixed)
            c_low = (normed * vecs[layer, 3:4, :] + vecs[layer, 4:5, :]).astype(BF16)
            c_v[layer] = c_low
            put(layer, 5, "c", c_v).start()
            for index in range(hidden_count):
                span = slice(index * feature, (index + 1) * feature)
                u = mm(c_low, we[index][layer]) + be[layer, :, span]
                square = u * u
                th = jnp.tanh(TANH_SCALE * (u + 0.044715 * (square * u)))
                half = 0.5 * (1.0 + th)
                m_v[layer, :, span] = (u * half).astype(BF16)
                slope = half + 0.5 * u * (1.0 - th * th) * (
                    TANH_SCALE * (1.0 + 3.0 * 0.044715 * square)
                )
                d_v[layer, :, span] = slope.astype(BF16)
            put(layer, 6, "m", m_v).start()
            put(layer, 7, "d", d_v).start()
            z = vecs[layer, 5:6, :]
            for index in range(hidden_count):
                span = slice(index * feature, (index + 1) * feature)
                z = z + mm(m_v[layer, :, span], wc[index][layer])
            h_v[layer + 1] = mixed + branch_scale * z

        layer_loop(one_layer)
        sent[...] = h_v[LAYERS]

        @pl.when(last)
        def _():
            final = pltpu.make_async_copy(h_v.at[LAYERS], stash["f"].at[slot], in_sem.at[1])
            final.start()
            final.wait()

        for layer in range(LAYERS):
            for index, (name, value_ref) in enumerate(
                (
                    ("h", h_v),
                    ("g", g_v),
                    ("a", a_v),
                    ("t", t_v),
                    ("o", o_v),
                    ("c", c_v),
                    ("m", m_v),
                    ("d", d_v),
                )
            ):
                put(layer, index, name, value_ref).wait()


def counts_of(weights, feature):
    hidden_count = (len(weights) - 4) // 2
    return 3, hidden_count


def cost_of(length, weights):
    return pl.CostEstimate(
        flops=2 * length * sum(w.size for w in weights),
        bytes_accessed=2 * sum(w.size for w in weights),
        transcendentals=0,
    )


def forward_step(branch_scale, tick, tokens, arrived, allowed, weights, vectors, stash):
    length, feature = arrived.shape
    joint_count, hidden_count = counts_of(weights, feature)
    hidden = hidden_count * feature
    weights = tuple(pltpu.with_memory_space_constraint(w, pltpu.VMEM) for w in weights)
    scratch = [
        pltpu.VMEM((LAYERS + 1, length, feature), F32),
        pltpu.VMEM((LAYERS, length, feature), F32),
        pltpu.VMEM((LAYERS, length, feature), BF16),
        pltpu.VMEM((LAYERS, length, 3 * feature), BF16),
        pltpu.VMEM((LAYERS, length, feature), BF16),
        pltpu.VMEM((LAYERS, length, feature), BF16),
        pltpu.VMEM((LAYERS, length, hidden), BF16),
        pltpu.VMEM((LAYERS, length, hidden), BF16),
        pltpu.SemaphoreType.DMA((2,)),
        pltpu.SemaphoreType.DMA((LAYERS, 8)),
    ]
    leading = 4 + len(weights) + len(vectors)
    outs = pl.pallas_call(
        partial(forward_kernel, branch_scale, joint_count, hidden_count),
        out_shape=tuple(pltpu.HBM(s.shape, s.dtype) for s in stash)
        + (pltpu.VMEM((length, feature), F32), jax.ShapeDtypeStruct((1,), jnp.int32)),
        in_specs=[SMEM, ANY, ANY]
        + [VMEM] * (1 + len(weights) + len(vectors))
        + [HBM] * len(stash),
        out_specs=tuple([HBM] * len(stash) + [VMEM, SMEM]),
        scratch_shapes=scratch,
        input_output_aliases={leading + i: i for i in range(len(stash))},
        compiler_params=pltpu.CompilerParams(vmem_limit_bytes=SCOPED),
        cost_estimate=cost_of(length, weights),
        name="forward_step",
    )(tick, in_hbm(tokens), arrived, allowed, *weights, *vectors, *stash)
    return outs[:-2], outs[-2], outs[-1]


def backward_kernel(branch_scale, joint_count, hidden_count, tick, seeds, arrived, allowed_rows, *refs):
    weight_count = joint_count + 1 + 2 * hidden_count
    wj = refs[:joint_count]
    wo = refs[joint_count]
    we = refs[joint_count + 1 : joint_count + 1 + hidden_count]
    wc = refs[joint_count + 1 + hidden_count : weight_count]
    vecs, sh, sg, st, sd = refs[weight_count : weight_count + 5]
    refs = refs[weight_count + 5 :]
    names = ("gw", "gu", "gz", "gt", "small", "r")
    stash = dict(zip(names, refs[6:12]))
    sent, next_tick = refs[12:14]
    (
        h_v,
        g_v,
        t_v,
        d_v,
        grad_v,
        gw_v,
        gu_v,
        gz_v,
        go_v,
        gt_v,
        small_v,
        in_sem,
        s_sem,
        out_sem,
    ) = refs[14:]
    next_tick[0] = tick[0] + 1
    section = lax.axis_index("section")
    sections = lax.axis_size("section")
    _, length, feature = seeds.shape
    rows = allowed_rows.shape[0]
    row_index = tick[0] - 2 * (sections - 1 - section)

    @pl.when((row_index >= 0) & (row_index < rows))
    def _():
        slot = jnp.clip(row_index, 0, rows - 1)

        @pl.when(section == sections - 1)
        def _():
            pltpu.make_async_copy(seeds.at[lax.rem(slot, seeds.shape[0])], grad_v, in_sem.at[0]).start()

        @pl.when(section < sections - 1)
        def _():
            pltpu.make_async_copy(arrived, grad_v, in_sem.at[0]).start()

        saved = ((sd, d_v), (sg, g_v), (st, t_v), (sh, h_v))

        def saved_copy(layer, index):
            source, target = saved[index]
            return pltpu.make_async_copy(
                source.at[layer, slot], target.at[layer], s_sem.at[layer, index]
            )

        for layer in reversed(range(LAYERS)):
            for index in range(4):
                saved_copy(layer, index).start()

        def put(layer, index, name, value_ref):
            return pltpu.make_async_copy(
                value_ref.at[layer], stash[name].at[layer, slot], out_sem.at[layer, index]
            )

        allowed = jnp.concatenate([allowed_rows[slot], allowed_rows[slot]], axis=0) > 0.5
        pltpu.make_async_copy(arrived, grad_v, in_sem.at[0]).wait()

        def one_layer(turn):
            layer = LAYERS - 1 - turn
            gw = (branch_scale * grad_v[...]).astype(BF16)
            gw_v[layer] = gw
            put(layer, 0, "gw", gw_v).start()
            small_v[layer, 7:8, :] = column_sum(gw)
            saved_copy(layer, 0).wait()
            gc = jnp.zeros((length, feature), F32)
            for index in range(hidden_count):
                span = slice(index * feature, (index + 1) * feature)
                gu = (d_v[layer, :, span].astype(F32) * mm(gw, wc[index][layer])).astype(BF16)
                gu_v[layer, :, span] = gu
                small_v[layer, 8 + index : 9 + index, :] = column_sum(gu)
            put(layer, 1, "gu", gu_v).start()
            for index in range(hidden_count):
                span = slice(index * feature, (index + 1) * feature)
                gc = gc + mm(gu_v[layer, :, span], we[index][layer])
            saved_copy(layer, 1).wait()
            normed, scale = norm_parts(g_v[layer])
            small_v[layer, 4:5, :] = column_sum(gc * normed)
            small_v[layer, 5:6, :] = column_sum(gc)
            gg = grad_v[...] + norm_back(normed, scale, vecs[layer, 3:4, :], gc)
            grad_v[...] = gg
            gz = (branch_scale * gg).astype(BF16)
            gz_v[layer] = gz
            put(layer, 2, "gz", gz_v).start()
            small_v[layer, 6:7, :] = column_sum(gz)
            go_v[...] = mm(gz, wo[layer]).astype(BF16)
            saved_copy(layer, 2).wait()
            for start in range(0, feature, PAIR):
                queries = stack_halves(t_v[layer, :, start : start + PAIR])
                keys = t_v[layer, :, feature + start : feature + start + PAIR]
                values = t_v[layer, :, 2 * feature + start : 2 * feature + start + PAIR]
                go = stack_halves(go_v[:, start : start + PAIR])
                chances = pair_probabilities(queries, keys, allowed)
                g_values = mm_tn(chances.astype(BF16), go)
                g_chances = mm_nt(go, values)
                inner = jnp.sum(chances * g_chances, axis=-1, keepdims=True)
                g_scores = jnp.where(allowed, chances * (g_chances - inner), 0.0).astype(BF16)
                g_queries = join_halves(mm(g_scores, keys)) * HEAD_DIM ** (-0.5)
                g_keys = mm_tn(g_scores, queries) * HEAD_DIM ** (-0.5)
                for part, value in enumerate((g_queries, g_keys, g_values)):
                    low = part * feature + start
                    gt_v[layer, :, low : low + PAIR] = value.astype(BF16)
            put(layer, 3, "gt", gt_v).start()
            small_v[layer, 2:3, :] = column_sum(gt_v[layer, :, :feature])
            small_v[layer, 3:4, :] = column_sum(gt_v[layer, :, 2 * feature :])
            ga = jnp.zeros((length, feature), F32)
            for index in range(joint_count):
                span = slice(index * feature, (index + 1) * feature)
                ga = ga + mm(gt_v[layer, :, span], wj[index][layer])
            saved_copy(layer, 3).wait()
            normed, scale = norm_parts(h_v[layer])
            small_v[layer, 0:1, :] = column_sum(ga * normed)
            small_v[layer, 1:2, :] = column_sum(ga)
            grad_v[...] = grad_v[...] + norm_back(normed, scale, vecs[layer, 0:1, :], ga)
            put(layer, 4, "small", small_v).start()

        layer_loop(one_layer)
        sent[...] = grad_v[...]

        @pl.when(section == 0)
        def _():
            final = pltpu.make_async_copy(grad_v, stash["r"].at[slot], in_sem.at[1])
            final.start()
            final.wait()

        for layer in range(LAYERS):
            for index, (name, value_ref) in enumerate(
                (
                    ("gw", gw_v),
                    ("gu", gu_v),
                    ("gz", gz_v),
                    ("gt", gt_v),
                    ("small", small_v),
                )
            ):
                put(layer, index, name, value_ref).wait()


def backward_step(branch_scale, tick, seeds, arrived, allowed, weights, vecs, saved, stash):
    length, feature = arrived.shape
    joint_count, hidden_count = counts_of(weights, feature)
    hidden = hidden_count * feature
    weights = tuple(pltpu.with_memory_space_constraint(w, pltpu.VMEM) for w in weights)
    scratch = [
        pltpu.VMEM((LAYERS, length, feature), F32),
        pltpu.VMEM((LAYERS, length, feature), F32),
        pltpu.VMEM((LAYERS, length, 3 * feature), BF16),
        pltpu.VMEM((LAYERS, length, hidden), BF16),
        pltpu.VMEM((length, feature), F32),
        pltpu.VMEM((LAYERS, length, feature), BF16),
        pltpu.VMEM((LAYERS, length, hidden), BF16),
        pltpu.VMEM((LAYERS, length, feature), BF16),
        pltpu.VMEM((length, feature), BF16),
        pltpu.VMEM((LAYERS, length, 3 * feature), BF16),
        pltpu.VMEM((LAYERS, 16, feature), F32),
        pltpu.SemaphoreType.DMA((2,)),
        pltpu.SemaphoreType.DMA((LAYERS, 4)),
        pltpu.SemaphoreType.DMA((LAYERS, 5)),
    ]
    leading = 5 + len(weights) + len(saved)
    outs = pl.pallas_call(
        partial(backward_kernel, branch_scale, joint_count, hidden_count),
        out_shape=tuple(pltpu.HBM(s.shape, s.dtype) for s in stash)
        + (pltpu.VMEM((length, feature), F32), jax.ShapeDtypeStruct((1,), jnp.int32)),
        in_specs=[SMEM, ANY, ANY]
        + [VMEM] * (2 + len(weights))
        + [HBM] * (len(saved) + len(stash)),
        out_specs=tuple([HBM] * len(stash) + [VMEM, SMEM]),
        scratch_shapes=scratch,
        input_output_aliases={leading + i: i for i in range(len(stash))},
        compiler_params=pltpu.CompilerParams(vmem_limit_bytes=SCOPED),
        cost_estimate=cost_of(length, weights),
        name="backward_step",
    )(tick, in_hbm(seeds), arrived, allowed, *weights, vecs, *map(in_hbm, saved), *stash)
    return outs[:-2], outs[-2], outs[-1]


def empty_arrays(shapes):
    return pl.pallas_call(
        lambda *refs: None,
        out_shape=tuple(pltpu.HBM(s.shape, s.dtype) for s in shapes),
        out_specs=tuple([HBM] * len(shapes)),
        name="empty_arrays",
    )()


def body(
    tokens,
    cotangent,
    document_lengths,
    valid_counts,
    first_gain,
    first_shift,
    joint_weight,
    query_value_offsets,
    output_weight,
    output_bias,
    second_gain,
    second_shift,
    expand_weight,
    expand_bias,
    contract_weight,
    contract_bias,
):
    sections = lax.axis_size("section")
    replicas = lax.axis_size("dp")
    section = lax.axis_index("section")
    replica = lax.axis_index("dp")
    near = 2 if replicas % 2 == 0 else 1
    far = replicas // near
    group, member = replica // near, replica % near
    micro_count, row_count, length, feature = tokens.shape
    hidden = expand_weight.shape[-1]
    own = micro_count * row_count
    rows = own * far
    branch_scale = (LAYERS * sections) ** (-0.5)
    first, last = section == 0, section == sections - 1
    positions = jnp.arange(length, dtype=jnp.int32)

    lengths = document_lengths.reshape(own, -1)
    live = (positions[None] < valid_counts.reshape(own, 1)).astype(F32)
    edge_own = jnp.where(
        first,
        tokens.reshape(own, length, feature).astype(F32),
        cotangent.reshape(own, length, feature).astype(F32) * live[:, :, None],
    )
    edges, all_lengths = [edge_own], [lengths]
    for shift in range(1, far):
        pairs = [
            (((g + shift) % far) * near + m, g * near + m) for g in range(far) for m in range(near)
        ]
        ends = sorted({0, sections - 1})
        all_lengths.append(lax.ppermute(lengths, "dp", pairs))
        edges.append(
            lax.ppermute(
                edge_own,
                ("section", "dp"),
                [(e * replicas + a, e * replicas + b) for e in ends for a, b in pairs],
            )
        )
    document_ends = jnp.cumsum(jnp.concatenate(all_lengths, axis=0), axis=-1)
    segment = jnp.sum(
        (positions[None, :, None] >= document_ends[:, None, :]).astype(jnp.int32), axis=-1
    )
    causal = positions[:, None] >= positions[None, :]
    allowed = ((segment[:, :, None] == segment[:, None, :]) & causal[None]).astype(F32)

    wide = [
        v.astype(F32)
        for v in (first_gain, first_shift, output_bias, second_gain, second_shift, contract_bias)
    ]
    blank = jnp.zeros_like(wide[0])
    vecs = jnp.stack(wide + [blank, blank], axis=1)
    offsets = query_value_offsets.astype(F32)
    bj = jnp.concatenate([offsets[:, :feature], blank, offsets[:, feature:]], axis=1)[:, None]
    be = expand_bias.astype(F32)[:, None]
    weights = (joint_weight, output_weight, expand_weight, contract_weight)

    def saved(width, dtype):
        return jax.ShapeDtypeStruct((LAYERS, rows, length, width), dtype)

    edge_shape = jax.ShapeDtypeStruct((rows, length, feature), F32)
    row_shape = jax.ShapeDtypeStruct((length, feature), F32)
    forward_shapes = (
        saved(feature, F32),
        saved(feature, F32),
        saved(feature, BF16),
        saved(3 * feature, BF16),
        saved(feature, BF16),
        saved(feature, BF16),
        saved(hidden, BF16),
        saved(hidden, BF16),
        edge_shape,
    )
    backward_shapes = (
        saved(feature, BF16),
        saved(hidden, BF16),
        saved(feature, BF16),
        saved(3 * feature, BF16),
        jax.ShapeDtypeStruct((LAYERS, rows, 16, feature), F32),
        edge_shape,
    )
    width = output_weight.shape[-1]
    turned_shape = jax.ShapeDtypeStruct(
        (len(weight_blocks(weights)), LAYERS, width, width), BF16
    )
    made = empty_arrays(forward_shapes + backward_shapes + (turned_shape, row_shape, row_shape))
    forward_stash = made[: len(forward_shapes)]
    backward_stash = made[len(forward_shapes) : -3]
    ticks = rows + 2 * (sections - 1)
    onward = [(i, i + 1) for i in range(sections - 1)]
    back = [(i + 1, i) for i in range(sections - 1)]

    steps = []
    while not steps or steps[-1] > 1:
        steps.append(steps[-1] // 2 if steps else sections // 2)
    mirrored = sections - 1 - section
    even = section % 2 == 0
    arrives = [jnp.where(even, section, mirrored) % (2 * step) == step for step in steps]
    vectors, allowed, even, arrives, first, where, weights = lax.optimization_barrier(
        ((vecs, bj, be), allowed, even, arrives, first, (section, group, member), weights)
    )
    turned = turn_weights(weights, made[-3], jnp.zeros((1,), jnp.int32), False)
    weights, turned = lax.optimization_barrier((weights, turned))
    loaded = load_weights(weights)
    chunk = min(ticks, UNROLL)
    rounds = -(-ticks // chunk)
    edge = jnp.concatenate(edges, axis=0) if rounds > 1 else None

    def halve(block, step):
        low, high = jnp.split(block, 2, axis=-1)
        pairs = [(a, a + step) for a in range(0, sections, 2 * step)]
        pairs += [(sections - 1 - a, sections - 1 - b) for a, b in pairs]
        got = lax.ppermute(jnp.where(even, high, low), "section", pairs)
        return jnp.where(even, low, high), got

    def spread(block, level):
        kept, got = halve(block, steps[level])
        if steps[level] == 1:
            return kept, got
        return jnp.where(arrives[level], got, kept)

    def run(step, pairs, stash):
        def turn(carry, source_of):
            stash, sent, arrived, tick = carry
            for index in range(chunk):
                idle = rounds == 1 and index == 0
                arriving = arrived if idle else lax.ppermute(sent, "section", pairs)
                stash, sent, tick = step(tick, source_of(index), arrived, stash)
                arrived = arriving
            return stash, sent, arrived, tick

        start = (stash, made[-2], made[-1], jnp.zeros((1,), jnp.int32))
        if rounds == 1:
            return turn(start, lambda index: edges[min(index, rows - 1) // own])[::3]

        def again(_, carry):
            return turn(carry, lambda index: edge)

        return lax.fori_loop(0, rounds, again, start)[::3]

    forward_stash, walked = run(
        lambda tick, source, arrived, stash: forward_step(
            branch_scale, tick, source, arrived, allowed, loaded, vectors, stash
        ),
        onward,
        forward_stash,
    )
    sh, sg, sa, st, so, sc, sm, sd, final_rows = forward_stash
    loaded = load_turned(turn_weights(weights, turned, walked, True))
    backward_stash, walked = run(
        lambda tick, source, arrived, stash: backward_step(
            branch_scale, tick, source, arrived, allowed, loaded, vectors[0], (sh, sg, st, sd), stash
        ),
        back,
        backward_stash,
    )
    backward_stash, (section, group, member), _ = lax.optimization_barrier(
        (backward_stash, where, walked)
    )
    gw, gu, gz, gt, small, first_rows = backward_stash

    def exchange(sends):
        got = []
        for shift, payload in enumerate(sends, 1):
            pairs = [
                (g * near + m, g * near + (m + shift) % near)
                for g in range(far)
                for m in range(near)
            ]
            got.append(lax.ppermute(payload, "dp", pairs))
        return got

    def near_sum(part):
        sends = [part((member + shift) % near) for shift in range(1, near)]
        return sends, lambda got: sum(got, part(member))

    def weight_gradient(left, right):
        width = left.shape[-1]
        share = width // replicas
        left = left.reshape(LAYERS, rows * length, width)
        right = right.reshape(LAYERS, rows * length, right.shape[-1])

        def part(index):
            mine = lax.dynamic_slice_in_dim(left, (group * near + index) * share, share, axis=2)
            return jnp.einsum("lrd,lre->lde", mine, right, preferred_element_type=F32)

        return near_sum(part)

    block = jnp.where(first, first_rows[:own], final_rows[:own])
    pending = []
    for level, (left, right) in enumerate(((sm, gw), (sc, gu), (sa, gt), (so, gz))):
        if level < len(steps):
            block = spread(block, level)
        sends, finish = weight_gradient(left, right)
        if level < len(steps):
            block, sends = lax.optimization_barrier((block, sends))
        pending.append((sends, finish))
    for level in range(len(pending), len(steps)):
        block = spread(block, level)
    kept, got = block
    pending = [finish(exchange(sends)) for sends, finish in pending]
    contract_gradient, expand_gradient, joint_gradient, output_gradient = pending

    sums = jnp.sum(small, axis=1)
    vectors = [
        sums[:, 0],
        sums[:, 1],
        sums[:, 2:4].reshape(LAYERS, 2 * feature),
        sums[:, 6],
        sums[:, 4],
        sums[:, 5],
        sums[:, 8 : 8 + hidden // feature].reshape(LAYERS, hidden),
        sums[:, 7],
    ]
    packed = jnp.concatenate([v.reshape(LAYERS, replicas, -1) for v in vectors], axis=2)
    sends, finish = near_sum(
        lambda index: lax.dynamic_index_in_dim(
            packed, group * near + index, axis=1, keepdims=False
        )
    )
    shared = finish(exchange(sends))
    pieces, at = [], 0
    for v in vectors:
        share = v.shape[1] // replicas
        pieces.append(shared[:, at : at + share])
        at += share

    share = feature // sections
    out_shape = (micro_count, row_count, length, share)
    input_gradient = jnp.where(even, kept, got)
    final_hidden = jnp.where(even, got, kept)
    return (
        final_hidden.reshape(out_shape),
        input_gradient.reshape(out_shape),
        pieces[0],
        pieces[1],
        joint_gradient,
        pieces[2],
        output_gradient,
        pieces[3],
        pieces[4],
        pieces[5],
        expand_gradient,
        pieces[6],
        contract_gradient,
        pieces[7],
    )


def solution(mesh):
    return jax.shard_map(
        body,
        mesh=mesh,
        in_specs=(
            P(None, "dp", None, None),
            P(None, "dp", None, None),
            P(None, "dp", None),
            P(None, "dp"),
            P("section", None),
            P("section", None),
            P("section", None, None),
            P("section", None),
            P("section", None, None),
            P("section", None),
            P("section", None),
            P("section", None),
            P("section", None, None),
            P("section", None),
            P("section", None, None),
            P("section", None),
        ),
        out_specs=(
            P(None, "dp", None, "section"),
            P(None, "dp", None, "section"),
            P("section", "dp"),
            P("section", "dp"),
            P("section", "dp", None),
            P("section", "dp"),
            P("section", "dp", None),
            P("section", "dp"),
            P("section", "dp"),
            P("section", "dp"),
            P("section", "dp", None),
            P("section", "dp"),
            P("section", "dp", None),
            P("section", "dp"),
        ),
        check_vma=False,
    )
```
